32 devices in a mesh: dir: 2 (over x), gx: 16 (over z, y, core).
Axes of the slice: x: 2, y: 2, z: 4, core: 2. Of those that a mesh axis runs over, the one named last changes fastest.
Arguments:
- pops: float32 [19, 128, 64, 128], P(None, ('dir', 'gx')), parts along dimension 1, may hold values from 0.5 to 1.5
- heights: int32 [128, 128], P(('dir', 'gx')), parts along dimension 0, may hold values from 0 to 32
Outputs:
- pops_out: float32 [19, 128, 64, 128], P(None, ('dir', 'gx')), parts along dimension 1
The draws below stay inside these ranges and needn't reach their ends.
There are 2 independent parts, one for each index of `dir`. The reference program is written for one: setup_inputs(seed, part) draws one part's arguments, and reference() takes and returns one part's arrays. A program takes and returns all parts, laid end to end along the dimension named above; each array names one. Nothing has to cross between parts.
All inputs are finite; a program needn't handle non-finite values.
Results may differ from the reference program's by a relative error of at most 0.0003.
Values sent between devices are 32-bit elements; how exact they have to be, the bound alone decides.
No kernel may reach another device: no remote copies, remote signals or barrier semaphores. Data moves between devices by JAX's collectives and lax.ppermute only.
A program may use at most 64 MiB of HBM per device.

```python
import jax
import jax.numpy as jnp
from jax import lax

Q = 19
NY = 128
NZ = 64
STEPS = 6
NX = 64


def place_ends(drawn, own_key, smallest, high):
    longest = drawn.shape.index(max(drawn.shape))
    spots = []
    for shift in (0, 1):
        where = [jax.random.randint(jax.random.fold_in(own_key, axis), (), 0, length) for axis, length in enumerate(drawn.shape)]
        where[longest] = (where[longest] + shift) % drawn.shape[longest]
        spots.append(tuple(where))
    return drawn.at[spots[0]].set(smallest).at[spots[1]].set(high)


def shard_levels(rng, shape, shards, smallest, high):
    def one(position, parts):
        steps = jax.random.uniform(jax.random.fold_in(jax.random.fold_in(rng, 6), position), (parts,), jnp.float32, smallest / len(shards), high / len(shards))
        return jnp.repeat(jnp.exp(steps), shape[position] // parts).reshape((-1,) + (1,) * (len(shape) - position - 1))

    loudness = one(*shards[0])
    for cut in shards[1:]:
        loudness = loudness * one(*cut)
    return loudness


def setup_inputs(seed: int = 0, part: int = 0) -> dict:
    arg_keys = jax.random.split(jax.random.key(seed), 3)
    part_splits = jax.random.split(jax.random.fold_in(arg_keys[2], part), 3)
    return {
        "pops": jnp.clip(0.5 + 1.0 * jax.random.uniform(part_splits[0], (Q, NX, NZ, NY), jnp.float32) ** shard_levels(part_splits[0], (Q, NX, NZ, NY), ((1, 16),), -0.2, 0.2), 0.5, 1.5),
        "heights": place_ends(jax.random.randint(part_splits[1], (NX, NY), 0, NZ // 2 + 1), jax.random.fold_in(part_splits[1], 1), 0, (NZ // 2 + 1) - 1).astype(jnp.int32),
    }


velocity_table = [(0, 0, 0), (1, 0, 0), (-1, 0, 0), (0, 1, 0), (0, -1, 0), (0, 0, 1), (0, 0, -1),
                  (1, 1, 0), (-1, -1, 0), (1, -1, 0), (-1, 1, 0), (1, 0, 1), (-1, 0, -1), (1, 0, -1), (-1, 0, 1),
                  (0, 1, 1), (0, -1, -1), (0, 1, -1), (0, -1, 1)]
weight_table = [1.0 / 3.0] + [1.0 / 18.0] * 6 + [1.0 / 36.0] * 12
omega_rate = 1.9


def opposite(component):
    if component == 0:
        return 0
    return component + 1 if component % 2 == 1 else component - 1


def collide(populations):
    density = jnp.zeros_like(populations[0])
    moment_x = jnp.zeros_like(populations[0])
    moment_y = jnp.zeros_like(populations[0])
    moment_z = jnp.zeros_like(populations[0])
    for component in range(19):
        step_x, step_y, step_z = velocity_table[component]
        term = weight_table[component] * populations[component]
        density = density + term
        if step_x != 0:
            moment_x = moment_x + step_x * term
        if step_y != 0:
            moment_y = moment_y + step_y * term
        if step_z != 0:
            moment_z = moment_z + step_z * term
    speed_x = moment_x / density
    speed_y = moment_y / density
    speed_z = moment_z / density
    speed_sq = speed_x * speed_x + speed_y * speed_y + speed_z * speed_z
    result = []
    for component in range(19):
        step_x, step_y, step_z = velocity_table[component]
        along = step_x * speed_x + step_y * speed_y + step_z * speed_z
        equil = density * (1.0 + 3.0 * along + 4.5 * along * along - 1.5 * speed_sq)
        result.append(populations[component] + omega_rate * (equil - populations[component]))
    return result


def shift_cells(field, step_x, step_z, step_y, fill):
    moved = jnp.roll(field, (step_x, step_y), axis=(0, 2))
    if step_z == 1:
        moved = jnp.concatenate([jnp.full_like(moved[:, :1], fill), moved[:, :-1]], axis=1)
    elif step_z == -1:
        moved = jnp.concatenate([moved[:, 1:], jnp.full_like(moved[:, :1], fill)], axis=1)
    return moved


def reference(pops, heights):
    shape = pops.shape[1:]
    zcoord = lax.broadcasted_iota(jnp.int32, shape, 1)
    fluid = (zcoord >= heights[:, None, :]).astype(jnp.float32)
    current = [pops[component] for component in range(19)]
    for step_count in range(STEPS):
        post = collide(current)
        current = []
        for component in range(19):
            step_x, step_y, step_z = velocity_table[component]
            source_fluid = shift_cells(fluid, step_x, step_z, step_y, 0.0)
            moved = shift_cells(post[component], step_x, step_z, step_y, 0.0)
            current.append(jnp.where(source_fluid > 0.5, moved, post[opposite(component)]))
    return jnp.stack(current)
```

```python
import functools

import jax
import jax.numpy as jnp
from jax import lax
from jax.experimental import pallas as pl
from jax.experimental.pallas import tpu as pltpu
from jax.sharding import PartitionSpec as P

STEPS = 6
Q = 19
SUB = 8

velocity_table = [
    (0, 0, 0),
    (1, 0, 0),
    (-1, 0, 0),
    (0, 1, 0),
    (0, -1, 0),
    (0, 0, 1),
    (0, 0, -1),
    (1, 1, 0),
    (-1, -1, 0),
    (1, -1, 0),
    (-1, 1, 0),
    (1, 0, 1),
    (-1, 0, -1),
    (1, 0, -1),
    (-1, 0, 1),
    (0, 1, 1),
    (0, -1, -1),
    (0, 1, -1),
    (0, -1, 1),
]
W0, W1, W2 = 1.0 / 3.0, 1.0 / 18.0, 1.0 / 36.0
OMEGA = 1.9
KEEP = OMEGA - 1.0
PLUS = [1, 7, 9, 11, 13]
MINUS = [2, 8, 10, 12, 14]
FLAT = [0, 3, 4, 5, 6, 15, 16, 17, 18]
NP = len(PLUS)


def opp(i):
    if i == 0:
        return 0
    return i + 1 if i % 2 == 1 else i - 1


def sums_plus(g):
    a, b, c, d, e = g
    x = W1 * a + W2 * ((b + c) + (d + e))
    return x, W2 * (b - c), W2 * (d - e)


def sums_flat(g):
    g0, g3, g4, g5, g6, g15, g16, g17, g18 = g
    s15, s17 = g15 + g16, g17 + g18
    d15, d17 = g15 - g16, g17 - g18
    rho = W0 * g0 + W1 * ((g3 + g4) + (g5 + g6)) + W2 * (s15 + s17)
    my = W1 * (g3 - g4) + W2 * (d15 + d17)
    mz = W1 * (g5 - g6) + W2 * (d15 - d17)
    return rho, my, mz


def equilibrium(rho, mx, my, mz):
    inv = 1.0 / rho
    k = 3.0 * OMEGA
    m = (mx * k, my * k, mz * k)
    half = inv * (1.5 / k)
    v = (m[0] * half, m[1] * half, m[2] * half)
    mv = m[0] * v[0] + m[1] * v[1] + m[2] * v[2]
    base = OMEGA * rho - mv * (1.0 / 3.0)
    return m, v, base


def along(c, m):
    total = None
    for step, value in zip(c, m):
        if step:
            if total is None:
                total = value if step == 1 else -value
            else:
                total = total + value if step == 1 else total - value
    return total


def collide_all(g):
    sp = sums_plus([g[i] for i in PLUS])
    sm = sums_plus([g[i] for i in MINUS])
    rho, my, mz = sums_flat([g[i] for i in FLAT])
    rho = rho + (sp[0] + sm[0])
    mx = sp[0] - sm[0]
    my = my + (sp[1] - sm[1])
    mz = mz + (sp[2] - sm[2])
    m, v, base = equilibrium(rho, mx, my, mz)
    post = [None] * Q
    post[0] = base - KEEP * g[0]
    for i in range(1, Q, 2):
        cm, cv = along(velocity_table[i], m), along(velocity_table[i], v)
        even = base + cm * cv
        post[i] = (even + cm) - KEEP * g[i]
        post[i + 1] = (even - cm) - KEEP * g[i + 1]
    return post


def collide_some(g, comps, rho, mx, my, mz):
    m, v, base = equilibrium(rho, mx, my, mz)
    post = []
    for value, i in zip(g, comps):
        first = i if i % 2 == 1 else i - 1
        cm, cv = along(velocity_table[first], m), along(velocity_table[first], v)
        even = base + cm * cv
        both = even + cm if i == first else even - cm
        post.append(both - KEEP * value)
    return post


class Field:
    def __init__(self, width, nz, edge, inner, low=None, high=None):
        self.width, self.nz = width, nz
        self.edge, self.inner, self.low, self.high = edge, inner, low, high

    def place(self, i, p):
        w, nz = self.width, self.nz
        if p == -1:
            ref, slot = self.low
            return ref, slot(i)
        if p == w:
            ref, slot = self.high
            return ref, slot(i)
        if p in (0, w - 1):
            return self.edge, SUB + (2 * i + (p != 0)) * nz
        return self.inner, SUB + (i * (w - 2) + p - 1) * nz

    def load(self, i, p, z, shift=0):
        ref, base = self.place(i, p)
        if shift == 0:
            return ref[pl.ds(pl.multiple_of(base + z, SUB), SUB), :]
        return ref[pl.ds(base + z - shift, SUB), :]

    def store(self, i, p, z, value):
        ref, base = self.place(i, p)
        ref[pl.ds(pl.multiple_of(base + z, SUB), SUB), :] = value


class Heights:
    def __init__(self, width, own, beside):
        self.width, self.own, self.beside = width, own, beside

    def get(self, p, roll):
        if p in (-1, self.width):
            row = (3 * (p != -1) + roll + 1) * SUB
            return self.beside[pl.ds(row, SUB), :]
        return self.own[pl.ds((3 * p + roll + 1) * SUB, SUB), :]


def roll_lanes(x, step):
    if step == 0:
        return x
    return pltpu.roll(x, step % x.shape[1], 1)


def levels(z, nz, ny):
    at = (lax.broadcasted_iota(jnp.int32, (SUB, ny), 0) + z).astype(jnp.float32)
    return {0: at, 1: at - 1.0, -1: jnp.where(at == nz - 1.0, -1.0, at + 1.0)}


def pull(field, heights, lev, i, p, z):
    cx, cy, cz = velocity_table[i]
    if i == 0:
        return field.load(0, p, z)
    moved = roll_lanes(field.load(i, p - cx, z, cz), cy)
    back = field.load(opp(i), p, z)
    return jnp.where(lev[cz] >= heights.get(p - cx, cy), moved, back)


def over_z(nz, body, unroll):
    blocks = nz // SUB

    def step(k, carry):
        body(pl.multiple_of(k * SUB, SUB))
        return carry

    lax.fori_loop(0, blocks, step, 0, unroll=min(unroll, blocks))


def first_edge_kernel(width, nz, pops, h, edge, up, down, own, buf, sem):
    ny = h.shape[1]
    copies = []
    for e, p in enumerate((0, width - 1)):
        copies.append(pltpu.make_async_copy(pops.at[:, p], buf.at[:, e], sem.at[e]))
        copies[-1].start()
    hf = h[...].astype(jnp.float32)
    for p in range(width):
        row = jnp.broadcast_to(hf[p : p + 1], (SUB, ny))
        for k in (-1, 0, 1):
            own[pl.ds((3 * p + k + 1) * SUB, SUB), :] = roll_lanes(row, k)
        if p == 0:
            down[pl.ds(NP * nz, SUB), :] = row
        if p == width - 1:
            up[pl.ds(NP * nz, SUB), :] = row
    field = Field(width, nz, edge, None)
    for c in copies:
        c.wait()

    def body(z):
        for e, p in enumerate((0, width - 1)):
            post = collide_all([buf[i, e, pl.ds(z, SUB), :] for i in range(Q)])
            for i in range(Q):
                field.store(i, p, z, post[i])
            send(post, p, width, nz, z, up, down)

    over_z(nz, body, UNROLL)


def send(post, p, width, nz, z, up, down):
    if p == 0:
        for k, i in enumerate(MINUS):
            down[pl.ds(pl.multiple_of(k * nz + z, SUB), SUB), :] = post[i]
    if p == width - 1:
        for k, i in enumerate(PLUS):
            up[pl.ds(pl.multiple_of(k * nz + z, SUB), SUB), :] = post[i]


def ahead(field, heights, lev, width, nz, z, up, down):
    for p, comps, out in ((width - 1, PLUS, up), (0, MINUS, down)):
        rows = [pull(field, heights, lev, i, p, z) for i in comps]
        rows += sums_flat([pull(field, heights, lev, i, p, z) for i in FLAT])
        for k, row in enumerate(rows):
            out[pl.ds(pl.multiple_of(k * nz + z, SUB), SUB), :] = row


def first_inner_kernel(width, nz, pops, own, edge, inner, up, down, buf, sem):
    ny = own.shape[1]
    copy = pltpu.make_async_copy(pops.at[:, 1 : width - 1], buf, sem)
    copy.start()
    field = Field(width, nz, edge, inner)
    heights = Heights(width, own, None)
    copy.wait()

    def body(z):
        for p in range(1, width - 1):
            post = collide_all([buf[i, p - 1, pl.ds(z, SUB), :] for i in range(Q)])
            for i in range(Q):
                field.store(i, p, z, post[i])

    over_z(nz, body, UNROLL)

    def body_ahead(z):
        ahead(field, heights, levels(z, nz, ny), width, nz, z, up, down)

    over_z(nz, body_ahead, UNROLL)


def inner_step(width, nz, field, new, heights, ny):
    def body(z):
        lev = levels(z, nz, ny)
        for p in range(1, width - 1):
            post = collide_all([pull(field, heights, lev, i, p, z) for i in range(Q)])
            for i in range(Q):
                new.store(i, p, z, post[i])

    over_z(nz, body, UNROLL)


def inner_kernel(width, nz, own, edge, inner, new_inner):
    field = Field(width, nz, edge, inner)
    inner_step(width, nz, field, Field(width, nz, None, new_inner), Heights(width, own, None), own.shape[1])


def inner_ahead_kernel(width, nz, own, edge, inner, new_edge, new_inner, up, down):
    ny = own.shape[1]
    heights = Heights(width, own, None)
    new = Field(width, nz, new_edge, new_inner)
    inner_step(width, nz, Field(width, nz, edge, inner), new, heights, ny)

    def body_ahead(z):
        ahead(new, heights, levels(z, nz, ny), width, nz, z, up, down)

    over_z(nz, body_ahead, UNROLL)


def slot_of(comps, nz, base=0):
    return lambda i: base + comps.index(i) * nz


def padded_low(nz, from_low, from_high, low, high):
    rows = NP * nz
    low[pl.ds(SUB, rows), :] = from_low[pl.ds(0, rows), :]
    high[pl.ds(SUB, rows), :] = from_high[pl.ds(0, rows), :]


def edge_kernel(first, width, nz, *refs):
    ny = refs[0].shape[1]
    if first:
        own, edge, inner, from_low, from_high, new_edge, sums_low, sums_high, beside, low, high = refs
        for s, ref in enumerate((from_low, from_high)):
            row = ref[pl.ds(NP * nz, SUB), :]
            for k in (-1, 0, 1):
                beside[pl.ds((3 * s + k + 1) * SUB, SUB), :] = roll_lanes(row, k)
    else:
        own, beside, edge, inner, from_low, from_high, new_edge, sums_low, sums_high, low, high = refs
    padded_low(nz, from_low, from_high, low, high)
    field = Field(
        width,
        nz,
        edge,
        inner,
        (low, slot_of(PLUS, nz, SUB)),
        (high, slot_of(MINUS, nz, SUB)),
    )
    heights = Heights(width, own, beside)
    new = Field(width, nz, new_edge, None)

    def body(z):
        lev = levels(z, nz, ny)
        for p in (0, width - 1):
            post = collide_all([pull(field, heights, lev, i, p, z) for i in range(Q)])
            for i in range(Q):
                new.store(i, p, z, post[i])
        for p, comps, out in ((-1, MINUS, sums_low), (width, PLUS, sums_high)):
            totals = sums_plus([pull(field, heights, lev, i, p, z) for i in comps])
            for k, row in enumerate(totals):
                out[pl.ds(pl.multiple_of(k * nz + z, SUB), SUB), :] = row

    over_z(nz, body, UNROLL)


def halo(nz, got, sums, sign, out):
    comps = PLUS if sign > 0 else MINUS

    def body(z):
        def row(ref, k):
            return ref[pl.ds(pl.multiple_of(k * nz + z, SUB), SUB), :]

        g = [row(got, k) for k in range(NP)]
        x, y1, z1 = sums_plus(g)
        x2, y2, z2 = (row(sums, k) for k in range(3))
        rho = row(got, NP) + (x + x2)
        mx = (x - x2) * sign if sign < 0 else x - x2
        my = row(got, NP + 1) + ((y1 - y2) if sign > 0 else (y2 - y1))
        mz = row(got, NP + 2) + ((z1 - z2) if sign > 0 else (z2 - z1))
        post = collide_some(g, comps, rho, mx, my, mz)
        for k in range(NP):
            out[pl.ds(pl.multiple_of(SUB + k * nz + z, SUB), SUB), :] = post[k]

    over_z(nz, body, UNROLL)


def halo_field(width, nz, edge, inner, got_low, got_high, sums_low, sums_high, low, high):
    halo(nz, got_low, sums_low, 1, low)
    halo(nz, got_high, sums_high, -1, high)
    return Field(
        width,
        nz,
        edge,
        inner,
        (low, slot_of(PLUS, nz, SUB)),
        (high, slot_of(MINUS, nz, SUB)),
    )


def next_edge_kernel(
    width, nz, own, beside, edge, inner, got_low, got_high, sums_low, sums_high, new_edge, up, down, low, high
):
    ny = own.shape[1]
    field = halo_field(width, nz, edge, inner, got_low, got_high, sums_low, sums_high, low, high)
    heights = Heights(width, own, beside)
    new = Field(width, nz, new_edge, None)

    def body(z):
        lev = levels(z, nz, ny)
        for p in (0, width - 1):
            post = collide_all([pull(field, heights, lev, i, p, z) for i in range(Q)])
            for i in range(Q):
                new.store(i, p, z, post[i])
            send(post, p, width, nz, z, up, down)

    over_z(nz, body, UNROLL)
    zero = jnp.zeros((SUB, ny), jnp.float32)
    up[pl.ds(NP * nz, SUB), :] = zero
    down[pl.ds(NP * nz, SUB), :] = zero


def write_planes(field, heights, nz, ny, planes, out, buf, sem):
    copies = []
    for k, p in enumerate(planes):

        def body(z, p=p, k=k):
            lev = levels(z, nz, ny)
            for i in range(Q):
                buf[i, k, pl.ds(z, SUB), :] = pull(field, heights, lev, i, p, z)

        over_z(nz, body, UNROLL)
        copies.append(pltpu.make_async_copy(buf.at[:, k], out.at[:, p], sem.at[k]))
        copies[-1].start()
    for c in copies:
        c.wait()


def last_inner_kernel(width, nz, own, edge, inner, out, buf, sem):
    field = Field(width, nz, edge, inner)
    write_planes(field, Heights(width, own, None), nz, own.shape[1], range(1, width - 1), out, buf, sem)


def last_edge_kernel(
    width,
    nz,
    own,
    beside,
    edge,
    inner,
    got_low,
    got_high,
    sums_low,
    sums_high,
    _,
    out,
    low,
    high,
    buf,
    sem,
):
    field = halo_field(width, nz, edge, inner, got_low, got_high, sums_low, sums_high, low, high)
    write_planes(field, Heights(width, own, beside), nz, own.shape[1], (0, width - 1), out, buf, sem)


UNROLL = 2
VMEM_LIMIT = 24 * 1024 * 1024


def per_device(pops, heights):
    _, width, nz, ny = pops.shape
    assert width >= 3 and nz % SUB == 0 and STEPS % 2 == 0
    devices = lax.axis_size("gx")
    to_up = [(i, (i + 1) % devices) for i in range(devices)]
    to_down = [(j, i) for i, j in to_up]

    def rows(n):
        return jax.ShapeDtypeStruct((n, ny), jnp.float32)

    vmem = pl.BlockSpec(memory_space=pltpu.VMEM)
    anywhere = pl.BlockSpec(memory_space=pl.ANY)
    edge_t = rows(Q * 2 * nz + 2 * SUB)
    inner_t = rows(Q * (width - 2) * nz + 2 * SUB)
    near_t = rows(NP * nz + SUB)
    far_t = rows((NP + 3) * nz)
    sums_t = rows(3 * nz)
    own_t = rows(3 * width * SUB)
    beside_t = rows(6 * SUB)
    halo_scratch = [pltpu.VMEM((NP * nz + 2 * SUB, ny), jnp.float32)] * 2

    def call(kernel, name, in_specs, outs, planes, scratch=(), out_specs=None, **kw):
        return pl.pallas_call(
            functools.partial(kernel, width, nz),
            out_shape=outs,
            in_specs=in_specs,
            out_specs=[vmem] * len(outs) if out_specs is None else out_specs,
            scratch_shapes=list(scratch),
            name=name,
            compiler_params=pltpu.CompilerParams(vmem_limit_bytes=VMEM_LIMIT),
            cost_estimate=pl.CostEstimate(
                flops=planes * nz * ny * 250, bytes_accessed=planes * nz * ny * 4 * Q * 2, transcendentals=0
            ),
            **kw,
        )

    def exchange(up, down):
        return lax.ppermute(up, "gx", to_up), lax.ppermute(down, "gx", to_down)

    dma = pltpu.SemaphoreType.DMA
    edge, up, down, own = call(
        first_edge_kernel,
        "first_edge",
        [anywhere, vmem],
        [edge_t, near_t, near_t, own_t],
        2,
        [pltpu.VMEM((Q, 2, nz, ny), jnp.float32), dma((2,))],
    )(pops, heights)
    near = exchange(up, down)
    inner, up, down = call(
        first_inner_kernel,
        "first_inner",
        [anywhere, vmem, vmem],
        [inner_t, far_t, far_t],
        width - 1,
        [pltpu.VMEM((Q, width - 2, nz, ny), jnp.float32), dma],
    )(pops, own, edge)
    far = exchange(up, down)
    beside = None
    for t in range(0, STEPS, 2):
        last = t + 2 == STEPS
        inner1 = call(inner_kernel, "inner", [vmem] * 3, [inner_t], width - 2)(own, edge, inner)[0]
        if t == 0:
            edge1, sums_low, sums_high, beside = call(
                functools.partial(edge_kernel, True),
                "edge_first",
                [vmem] * 5,
                [edge_t, sums_t, sums_t, beside_t],
                3,
                halo_scratch,
            )(own, edge, inner, *near)
        else:
            edge1, sums_low, sums_high = call(
                functools.partial(edge_kernel, False),
                "edge",
                [vmem] * 6,
                [edge_t, sums_t, sums_t],
                3,
                halo_scratch,
            )(own, beside, edge, inner, *near)
        if last:
            break
        edge, up, down = call(
            next_edge_kernel, "next_edge", [vmem] * 8, [edge_t, near_t, near_t], 3, halo_scratch
        )(own, beside, edge1, inner1, *far, sums_low, sums_high)
        near = exchange(up, down)
        inner, up, down = call(
            inner_ahead_kernel, "inner_ahead", [vmem] * 4, [inner_t, far_t, far_t], width - 1
        )(own, edge1, inner1, edge)
        far = exchange(up, down)
    out_t = jax.ShapeDtypeStruct(pops.shape, pops.dtype)
    out = call(
        last_inner_kernel,
        "last_inner",
        [vmem] * 3,
        [out_t],
        width - 2,
        [pltpu.VMEM((Q, width - 2, nz, ny), jnp.float32), dma((width - 2,))],
        out_specs=[anywhere],
    )(own, edge1, inner1)[0]
    return call(
        last_edge_kernel,
        "last_edge",
        [vmem] * 8 + [anywhere],
        [out_t],
        3,
        halo_scratch + [pltpu.VMEM((Q, 2, nz, ny), jnp.float32), dma((2,))],
        out_specs=[anywhere],
        input_output_aliases={8: 0},
    )(own, beside, edge1, inner1, *far, sums_low, sums_high, out)[0]


def solution(mesh):
    placed = (P(None, ("dir", "gx"), None, None), P(("dir", "gx"), None))
    return jax.shard_map(
        per_device,
        mesh=mesh,
        in_specs=placed,
        out_specs=P(None, ("dir", "gx"), None, None),
        check_vma=False,
    )
```

```python
import functools

import jax
import jax.numpy as jnp
from jax import lax
from jax.experimental import pallas as pl
from jax.experimental.pallas import tpu as pltpu
from jax.sharding import PartitionSpec as P


STEPS = 6
Q = 19
SUB = 8

velocity_table = [
    (0, 0, 0),
    (1, 0, 0),
    (-1, 0, 0),
    (0, 1, 0),
    (0, -1, 0),
    (0, 0, 1),
    (0, 0, -1),
    (1, 1, 0),
    (-1, -1, 0),
    (1, -1, 0),
    (-1, 1, 0),
    (1, 0, 1),
    (-1, 0, -1),
    (1, 0, -1),
    (-1, 0, 1),
    (0, 1, 1),
    (0, -1, -1),
    (0, 1, -1),
    (0, -1, 1),
]
W0, W1, W2 = 1.0 / 3.0, 1.0 / 18.0, 1.0 / 36.0
OMEGA = 1.9
KEEP = OMEGA - 1.0
PLUS = [1, 11, 13, 7, 9]
MINUS = [2, 12, 14, 8, 10]
FLAT = [0, 3, 4, 5, 6, 15, 16, 17, 18]
NP = len(PLUS)


def opp(i):
    if i == 0:
        return 0
    return i + 1 if i % 2 == 1 else i - 1


def sums_side(g):
    a, b, c, d, e = g
    return W1 * a + W2 * ((b + c) + (d + e)), W2 * (d - e), W2 * (b - c)


def sums_flat(g):
    g0, g3, g4, g5, g6, g15, g16, g17, g18 = g
    s15, s17 = g15 + g16, g17 + g18
    d15, d17 = g15 - g16, g17 - g18
    rho = W0 * g0 + W1 * ((g3 + g4) + (g5 + g6)) + W2 * (s15 + s17)
    my = W1 * (g3 - g4) + W2 * (d15 + d17)
    mz = W1 * (g5 - g6) + W2 * (d15 - d17)
    return rho, my, mz


def equilibrium(rho, mx, my, mz):
    inv = 1.0 / rho
    k = 3.0 * OMEGA
    m = (mx * k, my * k, mz * k)
    half = inv * (1.5 / k)
    v = (m[0] * half, m[1] * half, m[2] * half)
    mv = m[0] * v[0] + m[1] * v[1] + m[2] * v[2]
    base = OMEGA * rho - mv * (1.0 / 3.0)
    return m, v, base


def along(c, m):
    total = None
    for step, value in zip(c, m):
        if step:
            if total is None:
                total = value if step == 1 else -value
            else:
                total = total + value if step == 1 else total - value
    return total


def collide_all(g):
    sp = sums_side([g[i] for i in PLUS])
    sm = sums_side([g[i] for i in MINUS])
    rho, my, mz = sums_flat([g[i] for i in FLAT])
    rho = rho + (sp[0] + sm[0])
    mx = sp[0] - sm[0]
    my = my + (sp[1] - sm[1])
    mz = mz + (sp[2] - sm[2])
    m, v, base = equilibrium(rho, mx, my, mz)
    post = [None] * Q
    post[0] = base - KEEP * g[0]
    for i in range(1, Q, 2):
        cm, cv = along(velocity_table[i], m), along(velocity_table[i], v)
        even = base + cm * cv
        post[i] = (even + cm) - KEEP * g[i]
        post[i + 1] = (even - cm) - KEEP * g[i + 1]
    return post


class Field:
    def __init__(self, width, nz, edge=None, inner=None, ghost=None, near=None, far=None):
        self.width, self.nz = width, nz
        self.edge, self.inner, self.ghost, self.near, self.far = edge, inner, ghost, near, far

    def place(self, i, p):
        w, nz = self.width, self.nz
        if p in (-1, w) and self.ghost is not None:
            return self.ghost, (2 * i + (p == w)) * nz
        if p in (-2, -1):
            return (self.near if p == -1 else self.far)[0], PLUS.index(i) * nz
        if p in (w, w + 1):
            return (self.near if p == w else self.far)[1], MINUS.index(i) * nz
        if p in (0, w - 1):
            return self.edge, (2 * i + (p != 0)) * nz
        return self.inner, (i * (w - 2) + p - 1) * nz

    def load(self, i, p, z, shift=0):
        ref, base = self.place(i, p)
        if shift:
            return ref[pl.ds(base + z - shift, SUB), :]
        return rows_at(ref, base + z)

    def store(self, i, p, z, value):
        ref, base = self.place(i, p)
        put_rows(ref, base + z, value)


def rows_at(ref, row):
    return ref[pl.ds(pl.multiple_of(row, SUB), SUB), :]


def put_rows(ref, row, value):
    ref[pl.ds(pl.multiple_of(row, SUB), SUB), :] = value


class Heights:
    def __init__(self, width, own, beside=None):
        self.width, self.own, self.beside = width, own, beside

    def get(self, p, roll):
        if 0 <= p < self.width:
            return rows_at(self.own, (3 * p + roll + 1) * SUB)
        k = p + 2 if p < 0 else p - self.width + 2
        return rows_at(self.beside, (3 * k + roll + 1) * SUB)


def roll_lanes(x, step):
    if step == 0:
        return x
    return pltpu.roll(x, step % x.shape[1], 1)


def put_heights(ref, k, row):
    for roll in (-1, 0, 1):
        put_rows(ref, (3 * k + roll + 1) * SUB, roll_lanes(row, roll))


def levels(z, nz, ny):
    at = (lax.broadcasted_iota(jnp.int32, (SUB, ny), 0) + z).astype(jnp.float32)
    return {0: at, 1: at - 1.0, -1: jnp.where(at == nz - 1.0, -1.0, at + 1.0)}


def pull(field, heights, lev, i, p, z):
    cx, cy, cz = velocity_table[i]
    if i == 0:
        return field.load(0, p, z)
    moved = roll_lanes(field.load(i, p - cx, z, cz), cy)
    back = field.load(opp(i), p, z)
    return jnp.where(lev[cz] >= heights.get(p - cx, cy), moved, back)


def over_rows(rows, body):
    blocks = rows // SUB

    def step(k, carry):
        body(pl.multiple_of(k * SUB, SUB))
        return carry

    lax.fori_loop(0, blocks, step, 0, unroll=min(UNROLL, blocks))


def give(up, down, out_a, out_b):
    even = lax.rem(lax.axis_index("gx"), 2) == 0
    for cond, first, second in ((even, up, down), (jnp.logical_not(even), down, up)):

        @pl.when(cond)
        def _(first=first, second=second):
            def body(z):
                put_rows(out_a, z, rows_at(first, z))
                put_rows(out_b, z, rows_at(second, z))

            over_rows(up.shape[0], body)


def take(got_a, got_b, low, high):
    even = lax.rem(lax.axis_index("gx"), 2) == 0
    for cond, first, second in ((even, high, low), (jnp.logical_not(even), low, high)):

        @pl.when(cond)
        def _(first=first, second=second):
            def body(z):
                put_rows(first, z, rows_at(got_a, z))
                put_rows(second, z, rows_at(got_b, z))

            over_rows(low.shape[0], body)


def step_planes(field, new, heights, planes, nz, ny):
    def body(z):
        lev = levels(z, nz, ny)
        for p in planes:
            post = collide_all([pull(field, heights, lev, i, p, z) for i in range(Q)])
            for i in range(Q):
                new.store(i, p, z, post[i])

    over_rows(nz, body)


def give_second(inner, width, nz, out_a, out_b):
    field = Field(width, nz, None, inner)

    def copy(refs, p_up, p_down):
        def body(z):
            for k in range(NP):
                put_rows(refs[0], k * nz + z, field.load(PLUS[k], p_up, z))
                put_rows(refs[1], k * nz + z, field.load(MINUS[k], p_down, z))

        over_rows(nz, body)

    even = lax.rem(lax.axis_index("gx"), 2) == 0

    @pl.when(even)
    def _():
        copy((out_a, out_b), width - 2, 1)

    @pl.when(jnp.logical_not(even))
    def _():
        copy((out_b, out_a), width - 2, 1)


def edge0_kernel(width, nz, pops, h_hbm, edge, out_a, out_b, own, buf, h, up, down, sem):
    ny = h.shape[1]
    edges = (0, width - 1)
    copies = [pltpu.make_async_copy(pops.at[:, p], buf.at[:, e], sem.at[e]) for e, p in enumerate(edges)]
    copies.append(pltpu.make_async_copy(h_hbm, h, sem.at[2]))
    for c in copies:
        c.start()
    copies[2].wait()
    hf = h[...].astype(jnp.float32)
    for p in range(width):
        row = jnp.broadcast_to(hf[p : p + 1], (SUB, ny))
        put_heights(own, p, row)
        for out, first in ((down, 0), (up, width - 2)):
            if first <= p < first + 2:
                put_rows(out, NP * nz + (p - first) * SUB, row)
    field = Field(width, nz, edge)
    copies[0].wait()
    copies[1].wait()

    def body(z):
        for e, p in enumerate(edges):
            post = collide_all([buf[i, e, pl.ds(z, SUB), :] for i in range(Q)])
            for i in range(Q):
                field.store(i, p, z, post[i])
            for k in range(NP):
                if e:
                    put_rows(up, k * nz + z, post[PLUS[k]])
                else:
                    put_rows(down, k * nz + z, post[MINUS[k]])

    over_rows(nz, body)
    give(up, down, out_a, out_b)


def inner0_kernel(width, nz, pops, own, edge, inner, out_a, out_b, buf, up, down, sem):
    ny = own.shape[1]
    copy = pltpu.make_async_copy(pops.at[:, 1 : width - 1], buf, sem)
    copy.start()
    field = Field(width, nz, edge, inner)
    heights = Heights(width, own)
    copy.wait()

    def body(z):
        for p in range(1, width - 1):
            post = collide_all([buf[i, p - 1, pl.ds(z, SUB), :] for i in range(Q)])
            for i in range(Q):
                field.store(i, p, z, post[i])

    over_rows(nz, body)

    def body_ghost(z):
        lev = levels(z, nz, ny)
        for p, comps, out in ((width - 1, PLUS, up), (0, MINUS, down)):
            for k, i in enumerate(comps + FLAT):
                put_rows(out, k * nz + z, pull(field, heights, lev, i, p, z))

    over_rows(nz, body_ghost)
    give(up, down, out_a, out_b)


def inner1_kernel(width, nz, own, edge, inner, new_inner, out_a, out_b):
    ny = own.shape[1]
    new = Field(width, nz, None, new_inner)
    step_planes(Field(width, nz, edge, inner), new, Heights(width, own), range(1, width - 1), nz, ny)
    give_second(new_inner, width, nz, out_a, out_b)


def edge1_kernel(
    width, nz, own, edge0, inner0, inner1, got_a, got_b, edge1, inner2, out_a, out_b, beside, near_low, near_high
):
    ny = own.shape[1]
    take(got_a, got_b, near_low, near_high)
    for k in range(2):
        put_heights(beside, k, rows_at(near_low, NP * nz + k * SUB))
        put_heights(beside, k + 2, rows_at(near_high, NP * nz + k * SUB))
    heights = Heights(width, own, beside)
    old = Field(width, nz, edge0, inner0, near=(near_low, near_high))
    step_planes(old, Field(width, nz, edge1), heights, (0, width - 1), nz, ny)
    step_planes(Field(width, nz, edge1, inner1), Field(width, nz, None, inner2), heights, range(1, width - 1), nz, ny)
    give_second(inner2, width, nz, out_a, out_b)


def first_ghost(width, nz, ny, heights, edge0, near, got, ghost):
    old = Field(width, nz, edge0, near=near)
    new = Field(width, nz, ghost=ghost)

    def body(z):
        lev = levels(z, nz, ny)
        for p, known, own, ref in ((-1, PLUS, MINUS, got[0]), (width, MINUS, PLUS, got[1])):
            g = [None] * Q
            for k, i in enumerate(known + FLAT):
                g[i] = rows_at(ref, k * nz + z)
            for i in own:
                g[i] = pull(old, heights, lev, i, p, z)
            post = collide_all(g)
            for i in range(Q):
                new.store(i, p, z, post[i])

    over_rows(nz, body)


def write_planes(field, heights, nz, ny, planes, out, buf, sem):
    copies = []
    for k, p in enumerate(planes):

        def body(z, p=p, k=k):
            lev = levels(z, nz, ny)
            for i in range(Q):
                buf[i, k, pl.ds(z, SUB), :] = pull(field, heights, lev, i, p, z)

        over_rows(nz, body)
        copies.append(pltpu.make_async_copy(buf.at[:, k], out.at[:, p], sem.at[k]))
        copies[-1].start()
    return copies


def step_kernel(s, steps, width, nz, *refs):
    refs = list(refs)

    def pop(n):
        taken = refs[:n]
        del refs[:n]
        return taken

    own, beside, edge_old, edge, inner = pop(5)
    inner_next = pop(1)[0] if s + 2 <= steps else None
    extra = pop(2) if s == 1 else pop(1)
    got_a, got_b = pop(2)
    if s + 1 == steps:
        pop(1)
    ny = own.shape[1]
    heights = Heights(width, own, beside)
    ghost = edge_new = inner_new = out = out_a = out_b = None
    if s + 1 < steps:
        ghost, edge_new = pop(2)
    if s + 2 < steps:
        (inner_new,) = pop(1)
    else:
        (out,) = pop(1)
    if s + 3 < steps:
        out_a, out_b = pop(2)
    low, high = pop(2)
    if s + 1 == steps:
        (ghost,) = pop(1)
    take(got_a, got_b, low, high)
    if s == 1:
        first_ghost(width, nz, ny, heights, edge_old, extra, (low, high), ghost)
    else:
        old = Field(width, nz, edge_old, ghost=extra[0], far=(low, high))
        step_planes(old, Field(width, nz, ghost=ghost), heights, (-1, width), nz, ny)
    field = Field(width, nz, edge, inner, ghost)
    if s + 1 == steps:
        buf, sem = refs
        for c in write_planes(field, heights, nz, ny, (0, width - 1), out, buf, sem):
            c.wait()
        return
    step_planes(field, Field(width, nz, edge_new), heights, (0, width - 1), nz, ny)
    field = Field(width, nz, edge_new, inner_next)
    if s + 2 == steps:
        buf, sem = refs
        for c in write_planes(field, heights, nz, ny, range(1, width - 1), out, buf, sem):
            c.wait()
        return
    step_planes(field, Field(width, nz, None, inner_new), heights, range(1, width - 1), nz, ny)
    if s + 3 < steps:
        give_second(inner_new, width, nz, out_a, out_b)


UNROLL = 2
VMEM_LIMIT = 24 * 1024 * 1024


def per_device(pops, heights):
    _, width, nz, ny = pops.shape
    pops, heights = (pltpu.with_memory_space_constraint(x, pltpu.HBM) for x in (pops, heights))
    devices = lax.axis_size("gx")
    assert width >= 3 and nz % SUB == 0 and devices % 2 == 0 and STEPS >= 4
    pair_a = [(i, i ^ 1) for i in range(devices)]
    pair_b = [(i, (i + 1 if i % 2 else i - 1) % devices) for i in range(devices)]

    def rows(n):
        return jax.ShapeDtypeStruct((n, ny), jnp.float32)

    def scratch(n):
        return pltpu.VMEM((n, ny), jnp.float32)

    vmem = pl.BlockSpec(memory_space=pltpu.VMEM)
    hbm = pl.BlockSpec(memory_space=pltpu.HBM)
    edge_t = rows(Q * 2 * nz)
    inner_t = rows(Q * (width - 2) * nz)
    near_n = NP * nz + 2 * SUB
    set_n = (NP + len(FLAT)) * nz
    far_n = NP * nz
    dma = pltpu.SemaphoreType.DMA

    def call(kernel, args, outs, planes, scratch_shapes=(), in_specs=None, out_specs=None, **kw):
        return pl.pallas_call(
            functools.partial(kernel, width, nz),
            out_shape=outs,
            in_specs=[vmem] * len(args) if in_specs is None else in_specs,
            out_specs=[vmem] * len(outs) if out_specs is None else out_specs,
            scratch_shapes=list(scratch_shapes),
            compiler_params=pltpu.CompilerParams(vmem_limit_bytes=VMEM_LIMIT),
            cost_estimate=pl.CostEstimate(
                flops=planes * nz * ny * 250, bytes_accessed=planes * nz * ny * 4 * Q * 2, transcendentals=0
            ),
            **kw,
        )(*args)

    def exchange(a, b):
        a = lax.ppermute(a, "gx", pair_a)
        b = lax.ppermute(b, "gx", pair_b)
        return [a, b]

    edge0, a, b, own = call(
        edge0_kernel,
        [pops, heights],
        [edge_t, rows(near_n), rows(near_n), rows(3 * width * SUB)],
        2,
        [
            pltpu.VMEM((Q, 2, nz, ny), jnp.float32),
            pltpu.VMEM((width, ny), jnp.int32),
            scratch(near_n),
            scratch(near_n),
            dma((3,)),
        ],
        in_specs=[hbm, hbm],
    )
    near = exchange(a, b)
    inner0, a, b = call(
        inner0_kernel,
        [pops, own, edge0],
        [inner_t, rows(set_n), rows(set_n)],
        width,
        [pltpu.VMEM((Q, width - 2, nz, ny), jnp.float32), scratch(set_n), scratch(set_n), dma],
        in_specs=[hbm, vmem, vmem],
    )
    messages = {1: exchange(a, b)}
    inner1, a, b = call(inner1_kernel, [own, edge0, inner0], [inner_t, rows(far_n), rows(far_n)], width - 2)
    messages[2] = exchange(a, b)
    edge1, inner2, a, b, beside, low, high = call(
        edge1_kernel,
        [own, edge0, inner0, inner1, *near],
        [edge_t, inner_t, rows(far_n), rows(far_n), rows(12 * SUB), rows(near_n), rows(near_n)],
        width,
    )
    messages[3] = exchange(a, b)
    edges, inners, ghost = {0: edge0, 1: edge1}, {1: inner1, 2: inner2}, None
    out_t = jax.ShapeDtypeStruct(pops.shape, pops.dtype)
    out = None
    for s in range(1, STEPS):
        args = [own, beside, edges[s - 1], edges[s], inners[s]]
        if s + 2 <= STEPS:
            args.append(inners[s + 1])
        args += [low, high] if s == 1 else [ghost]
        args += messages[s]
        outs, spaces, aliases = [], [], {}
        n = set_n if s == 1 else far_n
        extra = [scratch(n), scratch(n)]
        specs = [vmem] * len(args)
        if s + 1 < STEPS:
            outs += [edge_t, edge_t]
        else:
            aliases = {len(args): 0}
            args.append(out)
            specs.append(hbm)
            extra.append(scratch(Q * 2 * nz))
        spaces = [vmem] * len(outs)
        if s + 2 < STEPS:
            outs.append(inner_t)
            spaces.append(vmem)
        else:
            outs.append(out_t)
            spaces.append(hbm)
            planes = 2 if s + 1 == STEPS else width - 2
            extra += [pltpu.VMEM((Q, planes, nz, ny), jnp.float32), dma((planes,))]
        if s + 3 < STEPS:
            outs += [rows(far_n), rows(far_n)]
            spaces += [vmem, vmem]
        got = list(call(
            functools.partial(step_kernel, s, STEPS),
            args,
            outs,
            width + 2,
            extra,
            in_specs=specs,
            out_specs=spaces,
            input_output_aliases=aliases,
        ))
        if s + 1 < STEPS:
            ghost, edges[s + 1] = got[0], got[1]
            del got[:2]
        if s + 2 < STEPS:
            inners[s + 2] = got[0]
        else:
            out = got[0]
        if s + 3 < STEPS:
            messages[s + 3] = exchange(got[1], got[2])
    return out


def solution(mesh):
    placed = (P(None, ("dir", "gx"), None, None), P(("dir", "gx"), None))

    return jax.shard_map(
        per_device,
        mesh=mesh,
        in_specs=placed,
        out_specs=P(None, ("dir", "gx"), None, None),
        check_vma=False,
    )
```

```python
import functools

import jax
import jax.numpy as jnp
from jax import lax
from jax.experimental import pallas as pl
from jax.experimental.pallas import tpu as pltpu
from jax.sharding import PartitionSpec as P


STEPS = 6
Q = 19
SUB = 8

velocity_table = [
    (0, 0, 0),
    (1, 0, 0),
    (-1, 0, 0),
    (0, 1, 0),
    (0, -1, 0),
    (0, 0, 1),
    (0, 0, -1),
    (1, 1, 0),
    (-1, -1, 0),
    (1, -1, 0),
    (-1, 1, 0),
    (1, 0, 1),
    (-1, 0, -1),
    (1, 0, -1),
    (-1, 0, 1),
    (0, 1, 1),
    (0, -1, -1),
    (0, 1, -1),
    (0, -1, 1),
]
OMEGA = 1.9
KEEP = OMEGA - 1.0
MAX_HEIGHT = 32
PLUS = [1, 11, 13, 7, 9]
MINUS = [2, 12, 14, 8, 10]
FLAT = [0, 3, 4, 5, 6, 15, 16, 17, 18]
REST = [4, 6, 15, 16, 17, 18]
NP = len(PLUS)


def opp(i):
    if i == 0:
        return 0
    return i + 1 if i % 2 == 1 else i - 1


def factors(t, steps):
    if t + 1 < steps:
        return None, -OMEGA / KEEP
    scale = (-1.0 / KEEP) ** t
    return -KEEP / scale, OMEGA / scale


def moments(g):
    s = {i: g[i] + g[i + 1] for i in range(1, Q, 2)}
    d = {i: g[i] - g[i + 1] for i in range(1, Q, 2)}
    axes = (s[1] + s[3]) + s[5]
    rho = (axes + axes) + ((s[7] + s[9]) + (s[11] + s[13])) + ((s[15] + s[17]) + g[0] * 12.0)
    x = (d[1] + d[1]) + ((d[7] + d[9]) + (d[11] + d[13]))
    y = (d[3] + d[3]) + ((d[7] - d[9]) + (d[15] + d[17]))
    z = (d[5] + d[5]) + ((d[11] - d[13]) + (d[15] - d[17]))
    return rho, x, y, z


def side_moments(g, comps):
    a, b, c, d, e = (g[i] for i in comps)
    rho = (a + a) + ((b + c) + (d + e))
    return (rho, d - e, b - c) if comps is PLUS else (rho, e - d, c - b)


def flat_moments(g):
    axes = (g[3] + g[4]) + (g[5] + g[6])
    rho = (axes + axes) + ((g[15] + g[16]) + (g[17] + g[18])) + g[0] * 12.0
    a, b, y, z = g[15] - g[16], g[17] - g[18], g[3] - g[4], g[5] - g[6]
    return rho, (y + y) + (a + b), (z + z) + (a - b)


def flat_from_rest(g, rho, y, z):
    a, b = g[15] - g[16], g[17] - g[18]
    g[3] = g[4] + (y - (a + b)) * 0.5
    g[5] = g[6] + (z - (a - b)) * 0.5
    axes = (g[3] + g[4]) + (g[5] + g[6])
    g[0] = (rho - (axes + axes) - ((g[15] + g[16]) + (g[17] + g[18]))) * (1.0 / 12.0)


def terms(rho, x, y, z, rate):
    half = 1.5 / rho
    mx, my, mz = (value * (rate / 12.0) for value in (x, y, z))
    vx, vy, vz = x * half, y * half, z * half
    xx, yy, zz = mx * vx, my * vy, mz * vz
    base = rho * (rate / 36.0) - ((xx + yy) + zz) * (1.0 / 3.0)
    ex, ey, ez = base + xx, base + yy, base + zz
    mx2, my2 = mx + mx, my + my
    exy, exz, eyz = ex + yy, ex + zz, ey + zz
    xy, xz, yz = mx2 * vy, mx2 * vz, my2 * vz
    return base, {
        1: (ex, mx),
        3: (ey, my),
        5: (ez, mz),
        7: (exy + xy, mx + my),
        9: (exy - xy, mx - my),
        11: (exz + xz, mx + mz),
        13: (exz - xz, mx - mz),
        15: (eyz + yz, my + mz),
        17: (eyz - yz, my - mz),
    }


def after(g, sums, t, steps, comps=range(Q)):
    keep, rate = factors(t, steps)
    base, parts = terms(*sums, rate)
    post = {}
    for i in comps:
        own = g[i] if keep is None else g[i] * keep
        if i == 0:
            post[i] = own + base
        elif i % 2:
            post[i] = own + (parts[i][0] + parts[i][1])
        else:
            post[i] = own + (parts[i - 1][0] - parts[i - 1][1])
    return post


def collide(g, t, steps):
    return after(g, moments(g), t, steps)


class Field:
    def __init__(self, width, nz, edge=None, inner=None, ghost=None, near=None, far=None, flats=None):
        self.width, self.nz = width, nz
        self.edge, self.inner, self.ghost, self.near, self.far, self.flats = edge, inner, ghost, near, far, flats

    def place(self, i, p):
        w, nz = self.width, self.nz
        if p in (-1, w) and self.flats is not None and i in FLAT:
            return self.flats, (2 * FLAT.index(i) + (p == w)) * nz
        if p in (-1, w) and self.ghost is not None:
            return self.ghost, (2 * i + (p == w)) * nz
        if p in (-2, -1):
            return (self.near if p == -1 else self.far)[0], PLUS.index(i) * nz
        if p in (w, w + 1):
            return (self.near if p == w else self.far)[1], MINUS.index(i) * nz
        if p in (0, w - 1):
            return self.edge, (2 * i + (p != 0)) * nz
        return self.inner, (i * (w - 2) + p - 1) * nz

    def load(self, i, p, z, shift=0):
        ref, base = self.place(i, p)
        if shift:
            return ref[pl.ds(base + z - shift, SUB), :]
        return rows_at(ref, base + z)

    def store(self, i, p, z, value):
        ref, base = self.place(i, p)
        put_rows(ref, base + z, value)


def rows_at(ref, row):
    return ref[pl.ds(pl.multiple_of(row, SUB), SUB), :]


def put_rows(ref, row, value):
    ref[pl.ds(pl.multiple_of(row, SUB), SUB), :] = value


class Heights:
    def __init__(self, width, own, beside=None):
        self.width, self.own, self.beside = width, own, beside

    def get(self, p, roll):
        if 0 <= p < self.width:
            return rows_at(self.own, (3 * p + roll + 1) * SUB)
        k = p + 2 if p < 0 else p - self.width + 2
        return rows_at(self.beside, (3 * k + roll + 1) * SUB)


def roll_lanes(x, step):
    if step == 0:
        return x
    return pltpu.roll(x, step % x.shape[1], 1)


def put_heights(ref, k, row):
    for roll in (-1, 0, 1):
        put_rows(ref, (3 * k + roll + 1) * SUB, roll_lanes(row, roll))


def levels(z, nz, ny):
    at = (lax.broadcasted_iota(jnp.int32, (SUB, ny), 0) + z).astype(jnp.float32)
    top = z + SUB == nz
    return {
        0: at,
        1: at - 1.0,
        -1: jnp.where(at == nz - 1.0, -1.0, at + 1.0) if top else at + 1.0,
        "inside": at < nz - 1.0 if top else None,
    }


def pull(field, heights, lev, i, p, z):
    cx, cy, cz = velocity_table[i]
    if i == 0:
        return field.load(0, p, z)
    moved = roll_lanes(field.load(i, p - cx, z, cz), cy)
    if z - cz < MAX_HEIGHT:
        fluid = lev[cz] >= heights.get(p - cx, cy)
    elif cz == -1 and lev["inside"] is not None:
        fluid = lev["inside"]
    else:
        return moved
    return jnp.where(fluid, moved, field.load(opp(i), p, z))


def over_rows(rows, body):
    for z in range(0, rows, SUB):
        body(z)


def give(up, down, out_a, out_b):
    even = lax.rem(lax.axis_index("gx"), 2) == 0
    for cond, first, second in ((even, up, down), (jnp.logical_not(even), down, up)):

        @pl.when(cond)
        def _(first=first, second=second):
            def body(z):
                put_rows(out_a, z, rows_at(first, z))
                put_rows(out_b, z, rows_at(second, z))

            over_rows(up.shape[0], body)


def take(got_a, got_b, low, high):
    even = lax.rem(lax.axis_index("gx"), 2) == 0
    for cond, first, second in ((even, high, low), (jnp.logical_not(even), low, high)):

        @pl.when(cond)
        def _(first=first, second=second):
            def body(z):
                put_rows(first, z, rows_at(got_a, z))
                put_rows(second, z, rows_at(got_b, z))

            over_rows(low.shape[0], body)


def step_planes(t, steps, field, new, heights, planes, nz, ny):
    def body(z):
        lev = levels(z, nz, ny)
        for p in planes:
            post = collide([pull(field, heights, lev, i, p, z) for i in range(Q)], t, steps)
            for i in range(Q):
                new.store(i, p, z, post[i])

    over_rows(nz, body)


def give_second(inner, width, nz, out_a, out_b, rest=None):
    field = Field(width, nz, None, inner)

    def copy(refs, p_up, p_down):
        def body(z):
            for k in range(NP):
                put_rows(refs[0], k * nz + z, field.load(PLUS[k], p_up, z))
                put_rows(refs[1], k * nz + z, field.load(MINUS[k], p_down, z))
            if rest is not None:
                for e, ref in enumerate(refs):
                    for k in range(len(REST)):
                        put_rows(ref, (NP + k) * nz + z, rows_at(rest, (e * len(REST) + k) * nz + z))

        over_rows(nz, body)

    even = lax.rem(lax.axis_index("gx"), 2) == 0

    @pl.when(even)
    def _():
        copy((out_a, out_b), width - 2, 1)

    @pl.when(jnp.logical_not(even))
    def _():
        copy((out_b, out_a), width - 2, 1)


def edge0_kernel(width, nz, pops, h_hbm, edge, out_a, out_b, own, buf, h, up, down, sem):
    ny = h.shape[1]
    edges = (0, width - 1)
    copies = [pltpu.make_async_copy(pops.at[:, p], buf.at[:, e], sem.at[e]) for e, p in enumerate(edges)]
    copies.append(pltpu.make_async_copy(h_hbm, h, sem.at[2]))
    for c in copies:
        c.start()
    copies[2].wait()
    hf = h[...].astype(jnp.float32)
    for p in range(width):
        row = jnp.broadcast_to(hf[p : p + 1], (SUB, ny))
        put_heights(own, p, row)
        for out, first in ((down, 0), (up, width - 2)):
            if first <= p < first + 2:
                put_rows(out, NP * nz + (p - first) * SUB, row)
    field = Field(width, nz, edge)
    copies[0].wait()
    copies[1].wait()

    def body(z):
        for e, p in enumerate(edges):
            post = collide([buf[i, e, pl.ds(z, SUB), :] for i in range(Q)], 0, STEPS)
            for i in range(Q):
                field.store(i, p, z, post[i])
            for k in range(NP):
                if e:
                    put_rows(up, k * nz + z, post[PLUS[k]])
                else:
                    put_rows(down, k * nz + z, post[MINUS[k]])

    over_rows(nz, body)
    give(up, down, out_a, out_b)


def inner0_kernel(width, nz, pops, own, edge, inner, out_a, out_b, rest, buf, up, down, sem):
    ny = own.shape[1]
    copy = pltpu.make_async_copy(pops.at[:, 1 : width - 1], buf, sem)
    copy.start()
    field = Field(width, nz, edge, inner)
    heights = Heights(width, own)
    copy.wait()

    def body(z):
        for p in range(1, width - 1):
            post = collide([buf[i, p - 1, pl.ds(z, SUB), :] for i in range(Q)], 0, STEPS)
            for i in range(Q):
                field.store(i, p, z, post[i])

    over_rows(nz, body)

    def body_ghost(z):
        lev = levels(z, nz, ny)
        for e, (p, comps, out) in enumerate(((width - 1, PLUS, up), (0, MINUS, down))):
            for k, i in enumerate(comps):
                put_rows(out, k * nz + z, pull(field, heights, lev, i, p, z))
            g = {i: pull(field, heights, lev, i, p, z) for i in FLAT}
            for k, row in enumerate(flat_moments(g)):
                put_rows(out, (NP + k) * nz + z, row)
            for k, i in enumerate(REST):
                put_rows(rest, (e * len(REST) + k) * nz + z, g[i])

    over_rows(nz, body_ghost)
    give(up, down, out_a, out_b)


def inner1_kernel(width, nz, own, edge, inner, rest, new_inner, out_a, out_b):
    ny = own.shape[1]
    new = Field(width, nz, None, new_inner)
    step_planes(1, STEPS, Field(width, nz, edge, inner), new, Heights(width, own), range(1, width - 1), nz, ny)
    give_second(new_inner, width, nz, out_a, out_b, rest)


def edge1_kernel(
    width, nz, own, edge0, inner0, inner1, got_a, got_b, edge1, inner2, out_a, out_b, beside, near_low, near_high
):
    ny = own.shape[1]
    take(got_a, got_b, near_low, near_high)
    for k in range(2):
        put_heights(beside, k, rows_at(near_low, NP * nz + k * SUB))
        put_heights(beside, k + 2, rows_at(near_high, NP * nz + k * SUB))
    heights = Heights(width, own, beside)
    old = Field(width, nz, edge0, inner0, near=(near_low, near_high))
    step_planes(1, STEPS, old, Field(width, nz, edge1), heights, (0, width - 1), nz, ny)
    both = Field(width, nz, edge1, inner1)
    step_planes(2, STEPS, both, Field(width, nz, None, inner2), heights, range(1, width - 1), nz, ny)
    give_second(inner2, width, nz, out_a, out_b)


def edge2_kernel(
    width,
    nz,
    own,
    beside,
    near_low,
    near_high,
    edge0,
    edge1,
    inner1,
    inner2,
    got_a,
    got_b,
    ghost1,
    sums,
    edge2,
    inner3,
    out_a,
    out_b,
    low,
    high,
):
    ny = own.shape[1]
    take(got_a, got_b, low, high)
    heights = Heights(width, own, beside)
    old = Field(width, nz, edge0, near=(near_low, near_high))
    ghost = Field(width, nz, ghost=ghost1)

    def body(z):
        lev = levels(z, nz, ny)
        for e, (p, known, mine, ref) in enumerate(((-1, PLUS, MINUS, low), (width, MINUS, PLUS, high))):
            g = {i: rows_at(ref, k * nz + z) for k, i in enumerate(known)}
            for i in mine:
                g[i] = pull(old, heights, lev, i, p, z)
            flat = [rows_at(ref, (NP + k) * nz + z) for k in range(3)]
            plus, minus = side_moments(g, PLUS), side_moments(g, MINUS)
            total = (
                flat[0] + (plus[0] + minus[0]),
                plus[0] - minus[0],
                flat[1] + (plus[1] + minus[1]),
                flat[2] + (plus[2] + minus[2]),
            )
            post = after(g, total, 1, STEPS, known + mine)
            for i in known + mine:
                ghost.store(i, p, z, post[i])
            for k, row in enumerate(total + tuple(flat)):
                put_rows(sums, (7 * e + k) * nz + z, row)

    over_rows(nz, body)
    step_planes(2, STEPS, Field(width, nz, edge1, inner1, ghost1), Field(width, nz, edge2), heights, (0, width - 1), nz, ny)
    both = Field(width, nz, edge2, inner2)
    step_planes(3, STEPS, both, Field(width, nz, None, inner3), heights, range(1, width - 1), nz, ny)
    give_second(inner3, width, nz, out_a, out_b)


def ghost_flats(width, nz, sums, low, high, flats):
    new = Field(width, nz, flats=flats)

    def body(z):
        for e, (p, ref) in enumerate(((-1, low), (width, high))):
            g = {i: rows_at(ref, (NP + k) * nz + z) for k, i in enumerate(REST)}
            row = [rows_at(sums, (7 * e + k) * nz + z) for k in range(7)]
            flat_from_rest(g, *row[4:])
            post = after(g, row[:4], 1, STEPS, FLAT)
            for i in FLAT:
                new.store(i, p, z, post[i])

    over_rows(nz, body)


def write_planes(field, heights, nz, ny, planes, out, buf, sem):
    copies = []
    for k, p in enumerate(planes):

        def body(z, p=p, k=k):
            lev = levels(z, nz, ny)
            for i in range(Q):
                buf[i, k, pl.ds(z, SUB), :] = pull(field, heights, lev, i, p, z)

        over_rows(nz, body)
        copies.append(pltpu.make_async_copy(buf.at[:, k], out.at[:, p], sem.at[k]))
        copies[-1].start()
    return copies


def step_kernel(s, steps, width, nz, *refs):
    refs = list(refs)

    def pop(n):
        taken = refs[:n]
        del refs[:n]
        return taken

    own, beside, edge_old, edge, inner = pop(5)
    inner_next = pop(1)[0] if s + 2 <= steps else None
    (ghost_old,) = pop(1)
    sums = pop(1)[0] if s == 2 else None
    got_a, got_b = pop(2)
    if s + 1 == steps:
        pop(1)
    ny = own.shape[1]
    heights = Heights(width, own, beside)
    ghost = edge_new = inner_new = out = out_a = out_b = None
    if s + 1 < steps:
        ghost, edge_new = pop(2)
    if s + 2 < steps:
        (inner_new,) = pop(1)
    else:
        (out,) = pop(1)
    if s + 3 < steps:
        out_a, out_b = pop(2)
    low, high = pop(2)
    if s + 1 == steps:
        (ghost,) = pop(1)
    take(got_a, got_b, low, high)
    flats = pop(1)[0] if s == 2 else None
    if s == 2:
        ghost_flats(width, nz, sums, low, high, flats)
    old = Field(width, nz, edge_old, ghost=ghost_old, far=(low, high), flats=flats)
    step_planes(s, steps, old, Field(width, nz, ghost=ghost), heights, (-1, width), nz, ny)
    field = Field(width, nz, edge, inner, ghost)
    if s + 1 == steps:
        buf, sem = refs
        for c in write_planes(field, heights, nz, ny, (0, width - 1), out, buf, sem):
            c.wait()
        return
    step_planes(s + 1, steps, field, Field(width, nz, edge_new), heights, (0, width - 1), nz, ny)
    field = Field(width, nz, edge_new, inner_next)
    if s + 2 == steps:
        buf, sem = refs
        for c in write_planes(field, heights, nz, ny, range(1, width - 1), out, buf, sem):
            c.wait()
        return
    step_planes(s + 2, steps, field, Field(width, nz, None, inner_new), heights, range(1, width - 1), nz, ny)
    if s + 3 < steps:
        give_second(inner_new, width, nz, out_a, out_b)


VMEM_LIMIT = 24 * 1024 * 1024


def per_device(pops, heights):
    _, width, nz, ny = pops.shape
    pops, heights = (pltpu.with_memory_space_constraint(x, pltpu.HBM) for x in (pops, heights))
    devices = lax.axis_size("gx")
    assert width >= 3 and nz % SUB == 0 and devices % 2 == 0 and STEPS >= 5
    pair_a = [(i, i ^ 1) for i in range(devices)]
    pair_b = [(i, (i + 1 if i % 2 else i - 1) % devices) for i in range(devices)]

    def rows(n):
        return jax.ShapeDtypeStruct((n, ny), jnp.float32)

    def scratch(n):
        return pltpu.VMEM((n, ny), jnp.float32)

    vmem = pl.BlockSpec(memory_space=pltpu.VMEM)
    hbm = pl.BlockSpec(memory_space=pltpu.HBM)
    edge_t = rows(Q * 2 * nz)
    inner_t = rows(Q * (width - 2) * nz)
    near_n = NP * nz + 2 * SUB
    sums_n = (NP + 3) * nz
    rest_n = (NP + len(REST)) * nz
    far_n = NP * nz
    dma = pltpu.SemaphoreType.DMA

    def call(kernel, args, outs, planes, scratch_shapes=(), in_specs=None, out_specs=None, **kw):
        return pl.pallas_call(
            functools.partial(kernel, width, nz),
            out_shape=outs,
            in_specs=[vmem] * len(args) if in_specs is None else in_specs,
            out_specs=[vmem] * len(outs) if out_specs is None else out_specs,
            scratch_shapes=list(scratch_shapes),
            compiler_params=pltpu.CompilerParams(vmem_limit_bytes=VMEM_LIMIT),
            cost_estimate=pl.CostEstimate(
                flops=planes * nz * ny * 250, bytes_accessed=planes * nz * ny * 4 * Q * 2, transcendentals=0
            ),
            **kw,
        )(*args)

    def exchange(a, b):
        a = lax.ppermute(a, "gx", pair_a)
        b = lax.ppermute(b, "gx", pair_b)
        return [a, b]

    edge0, a, b, own = call(
        edge0_kernel,
        [pops, heights],
        [edge_t, rows(near_n), rows(near_n), rows(3 * width * SUB)],
        2,
        [
            pltpu.VMEM((Q, 2, nz, ny), jnp.float32),
            pltpu.VMEM((width, ny), jnp.int32),
            scratch(near_n),
            scratch(near_n),
            dma((3,)),
        ],
        in_specs=[hbm, hbm],
    )
    near = exchange(a, b)
    inner0, a, b, rest = call(
        inner0_kernel,
        [pops, own, edge0],
        [inner_t, rows(sums_n), rows(sums_n), rows(2 * len(REST) * nz)],
        width,
        [pltpu.VMEM((Q, width - 2, nz, ny), jnp.float32), scratch(sums_n), scratch(sums_n), dma],
        in_specs=[hbm, vmem, vmem],
    )
    first = exchange(a, b)
    inner1, a, b = call(inner1_kernel, [own, edge0, inner0, rest], [inner_t, rows(rest_n), rows(rest_n)], width - 2)
    messages = {2: exchange(a, b)}
    edge1, inner2, a, b, beside, low, high = call(
        edge1_kernel,
        [own, edge0, inner0, inner1, *near],
        [edge_t, inner_t, rows(far_n), rows(far_n), rows(12 * SUB), rows(near_n), rows(near_n)],
        width,
    )
    messages[3] = exchange(a, b)
    ghost, sums, edge2, inner3, a, b = call(
        edge2_kernel,
        [own, beside, low, high, edge0, edge1, inner1, inner2, *first],
        [edge_t, rows(14 * nz), edge_t, inner_t, rows(far_n), rows(far_n)],
        width + 2,
        [scratch(sums_n), scratch(sums_n)],
    )
    messages[4] = exchange(a, b)
    edges, inners = {1: edge1, 2: edge2}, {2: inner2, 3: inner3}
    out_t = jax.ShapeDtypeStruct(pops.shape, pops.dtype)
    out = None
    for s in range(2, STEPS):
        args = [own, beside, edges[s - 1], edges[s], inners[s]]
        if s + 2 <= STEPS:
            args.append(inners[s + 1])
        args += [ghost, sums] if s == 2 else [ghost]
        args += messages[s]
        outs, spaces, aliases = [], [], {}
        n = rest_n if s == 2 else far_n
        extra = [scratch(n), scratch(n)]
        if s == 2:
            extra.append(scratch(2 * len(FLAT) * nz))
        specs = [vmem] * len(args)
        if s + 1 < STEPS:
            outs += [edge_t, edge_t]
        else:
            aliases = {len(args): 0}
            args.append(out)
            specs.append(hbm)
            extra.append(scratch(Q * 2 * nz))
        spaces = [vmem] * len(outs)
        if s + 2 < STEPS:
            outs.append(inner_t)
            spaces.append(vmem)
        else:
            outs.append(out_t)
            spaces.append(hbm)
            planes = 2 if s + 1 == STEPS else width - 2
            extra += [pltpu.VMEM((Q, planes, nz, ny), jnp.float32), dma((planes,))]
        if s + 3 < STEPS:
            outs += [rows(far_n), rows(far_n)]
            spaces += [vmem, vmem]
        got = list(call(
            functools.partial(step_kernel, s, STEPS),
            args,
            outs,
            width + 2,
            extra,
            in_specs=specs,
            out_specs=spaces,
            input_output_aliases=aliases,
        ))
        if s + 1 < STEPS:
            ghost, edges[s + 1] = got[0], got[1]
            del got[:2]
        if s + 2 < STEPS:
            inners[s + 2] = got[0]
        else:
            out = got[0]
        if s + 3 < STEPS:
            messages[s + 3] = exchange(got[1], got[2])
    return out


def solution(mesh):
    placed = (P(None, ("dir", "gx"), None, None), P(("dir", "gx"), None))

    return jax.shard_map(
        per_device,
        mesh=mesh,
        in_specs=placed,
        out_specs=P(None, ("dir", "gx"), None, None),
        check_vma=False,
    )
```

```python
import functools

import jax
import jax.numpy as jnp
from jax import lax
from jax.experimental import pallas as pl
from jax.experimental.pallas import tpu as pltpu
from jax.sharding import PartitionSpec as P


STEPS = 6
Q = 19
SUB = 8

velocity_table = [
    (0, 0, 0),
    (1, 0, 0),
    (-1, 0, 0),
    (0, 1, 0),
    (0, -1, 0),
    (0, 0, 1),
    (0, 0, -1),
    (1, 1, 0),
    (-1, -1, 0),
    (1, -1, 0),
    (-1, 1, 0),
    (1, 0, 1),
    (-1, 0, -1),
    (1, 0, -1),
    (-1, 0, 1),
    (0, 1, 1),
    (0, -1, -1),
    (0, 1, -1),
    (0, -1, 1),
]
OMEGA = 1.9
KEEP = OMEGA - 1.0
MAX_HEIGHT = 32
PLUS = [1, 11, 13, 7, 9]
MINUS = [2, 12, 14, 8, 10]
FLAT = [0, 3, 4, 5, 6, 15, 16, 17, 18]
REST = [4, 6, 15, 16, 17, 18]
NP = len(PLUS)


def opp(i):
    if i == 0:
        return 0
    return i + 1 if i % 2 == 1 else i - 1


def factors(t, steps):
    if t + 1 < steps:
        return None, -OMEGA / KEEP
    scale = (-1.0 / KEEP) ** t
    return -KEEP / scale, OMEGA / scale


def moments(g):
    s = {i: g[i] + g[i + 1] for i in range(1, Q, 2)}
    d = {i: g[i] - g[i + 1] for i in range(1, Q, 2)}
    axes = (s[1] + s[3]) + s[5]
    rho = (axes + axes) + ((s[7] + s[9]) + (s[11] + s[13])) + ((s[15] + s[17]) + g[0] * 12.0)
    x = (d[1] + d[1]) + ((d[7] + d[9]) + (d[11] + d[13]))
    y = (d[3] + d[3]) + ((d[7] - d[9]) + (d[15] + d[17]))
    z = (d[5] + d[5]) + ((d[11] - d[13]) + (d[15] - d[17]))
    return rho, x, y, z


def side_moments(g, comps):
    a, b, c, d, e = (g[i] for i in comps)
    rho = (a + a) + ((b + c) + (d + e))
    return (rho, d - e, b - c) if comps is PLUS else (rho, e - d, c - b)


def flat_moments(g):
    axes = (g[3] + g[4]) + (g[5] + g[6])
    rho = (axes + axes) + ((g[15] + g[16]) + (g[17] + g[18])) + g[0] * 12.0
    a, b, y, z = g[15] - g[16], g[17] - g[18], g[3] - g[4], g[5] - g[6]
    return rho, (y + y) + (a + b), (z + z) + (a - b)


def flat_from_rest(g, rho, y, z):
    a, b = g[15] - g[16], g[17] - g[18]
    g[3] = g[4] + (y - (a + b)) * 0.5
    g[5] = g[6] + (z - (a - b)) * 0.5
    axes = (g[3] + g[4]) + (g[5] + g[6])
    g[0] = (rho - (axes + axes) - ((g[15] + g[16]) + (g[17] + g[18]))) * (1.0 / 12.0)


def terms(rho, x, y, z, rate):
    half = 1.5 / rho
    mx, my, mz = (value * (rate / 12.0) for value in (x, y, z))
    vx, vy, vz = x * half, y * half, z * half
    xx, yy, zz = mx * vx, my * vy, mz * vz
    base = rho * (rate / 36.0) - ((xx + yy) + zz) * (1.0 / 3.0)
    ex, ey, ez = base + xx, base + yy, base + zz
    mx2, my2 = mx + mx, my + my
    exy, exz, eyz = ex + yy, ex + zz, ey + zz
    xy, xz, yz = mx2 * vy, mx2 * vz, my2 * vz
    return base, {
        1: (ex, mx),
        3: (ey, my),
        5: (ez, mz),
        7: (exy + xy, mx + my),
        9: (exy - xy, mx - my),
        11: (exz + xz, mx + mz),
        13: (exz - xz, mx - mz),
        15: (eyz + yz, my + mz),
        17: (eyz - yz, my - mz),
    }


def after(g, sums, t, steps, comps=range(Q)):
    keep, rate = factors(t, steps)
    base, parts = terms(*sums, rate)
    post = {}
    for i in comps:
        own = g[i] if keep is None else g[i] * keep
        if i == 0:
            post[i] = own + base
        elif i % 2:
            post[i] = own + (parts[i][0] + parts[i][1])
        else:
            post[i] = own + (parts[i - 1][0] - parts[i - 1][1])
    return post


def collide(g, t, steps):
    return after(g, moments(g), t, steps)


class Field:
    def __init__(self, width, nz, edge=None, inner=None, ghost=None, near=None, far=None, flats=None):
        self.width, self.nz = width, nz
        self.edge, self.inner, self.ghost, self.near, self.far, self.flats = edge, inner, ghost, near, far, flats

    def place(self, i, p):
        w, nz = self.width, self.nz
        if p in (-1, w) and self.flats is not None and i in FLAT:
            return self.flats, (2 * FLAT.index(i) + (p == w)) * nz
        if p in (-1, w) and self.ghost is not None:
            return self.ghost, (2 * i + (p == w)) * nz
        if p in (-2, -1):
            return (self.near if p == -1 else self.far)[0], PLUS.index(i) * nz
        if p in (w, w + 1):
            return (self.near if p == w else self.far)[1], MINUS.index(i) * nz
        if p in (0, w - 1):
            return self.edge, (2 * i + (p != 0)) * nz
        return self.inner, (i * (w - 2) + p - 1) * nz

    def load(self, i, p, z, shift=0):
        ref, base = self.place(i, p)
        if shift:
            return ref[pl.ds(base + z - shift, SUB), :]
        return rows_at(ref, base + z)

    def store(self, i, p, z, value):
        ref, base = self.place(i, p)
        put_rows(ref, base + z, value)


def rows_at(ref, row):
    return ref[pl.ds(pl.multiple_of(row, SUB), SUB), :]


def put_rows(ref, row, value):
    ref[pl.ds(pl.multiple_of(row, SUB), SUB), :] = value


class Heights:
    def __init__(self, width, own, beside=None):
        self.width, self.own, self.beside = width, own, beside

    def get(self, p, roll):
        if 0 <= p < self.width:
            return rows_at(self.own, (3 * p + roll + 1) * SUB)
        k = p + 2 if p < 0 else p - self.width + 2
        return rows_at(self.beside, (3 * k + roll + 1) * SUB)


def roll_lanes(x, step):
    if step == 0:
        return x
    return pltpu.roll(x, step % x.shape[1], 1)


def put_heights(ref, k, row):
    for roll in (-1, 0, 1):
        put_rows(ref, (3 * k + roll + 1) * SUB, roll_lanes(row, roll))


def levels(z, nz, ny):
    at = (lax.broadcasted_iota(jnp.int32, (SUB, ny), 0) + z).astype(jnp.float32)
    top = z + SUB == nz
    return {
        0: at,
        1: at - 1.0,
        -1: jnp.where(at == nz - 1.0, -1.0, at + 1.0) if top else at + 1.0,
        "inside": at < nz - 1.0 if top else None,
    }


def pull(field, heights, lev, i, p, z):
    cx, cy, cz = velocity_table[i]
    if i == 0:
        return field.load(0, p, z)
    moved = roll_lanes(field.load(i, p - cx, z, cz), cy)
    if z - cz < MAX_HEIGHT:
        fluid = lev[cz] >= heights.get(p - cx, cy)
    elif cz == -1 and lev["inside"] is not None:
        fluid = lev["inside"]
    else:
        return moved
    return jnp.where(fluid, moved, field.load(opp(i), p, z))


def over_rows(rows, body):
    for z in range(0, rows, SUB):
        body(z)


def give(up, down, out_a, out_b):
    even = lax.rem(lax.axis_index("gx"), 2) == 0
    for cond, first, second in ((even, up, down), (jnp.logical_not(even), down, up)):

        @pl.when(cond)
        def _(first=first, second=second):
            def body(z):
                put_rows(out_a, z, rows_at(first, z))
                put_rows(out_b, z, rows_at(second, z))

            over_rows(up.shape[0], body)


def take(got_a, got_b, low, high):
    even = lax.rem(lax.axis_index("gx"), 2) == 0
    for cond, first, second in ((even, high, low), (jnp.logical_not(even), low, high)):

        @pl.when(cond)
        def _(first=first, second=second):
            def body(z):
                put_rows(first, z, rows_at(got_a, z))
                put_rows(second, z, rows_at(got_b, z))

            over_rows(low.shape[0], body)


def step_planes(t, steps, field, new, heights, planes, nz, ny):
    def body(z):
        lev = levels(z, nz, ny)
        for p in planes:
            post = collide([pull(field, heights, lev, i, p, z) for i in range(Q)], t, steps)
            for i in range(Q):
                new.store(i, p, z, post[i])

    over_rows(nz, body)


def give_second(inner, width, nz, out_a, out_b, rest=None):
    field = Field(width, nz, None, inner)

    def copy(refs, p_up, p_down):
        def body(z):
            for k in range(NP):
                put_rows(refs[0], k * nz + z, field.load(PLUS[k], p_up, z))
                put_rows(refs[1], k * nz + z, field.load(MINUS[k], p_down, z))
            if rest is not None:
                for e, ref in enumerate(refs):
                    for k in range(len(REST)):
                        put_rows(ref, (NP + k) * nz + z, rows_at(rest, (e * len(REST) + k) * nz + z))

        over_rows(nz, body)

    even = lax.rem(lax.axis_index("gx"), 2) == 0

    @pl.when(even)
    def _():
        copy((out_a, out_b), width - 2, 1)

    @pl.when(jnp.logical_not(even))
    def _():
        copy((out_b, out_a), width - 2, 1)


def edge0_kernel(width, nz, pops, h_hbm, edge, out_a, out_b, own, buf, h, up, down, sem):
    ny = h.shape[1]
    edges = (0, width - 1)
    part = nz // HEAD_PARTS
    copies = []
    for k in range(HEAD_PARTS):
        rows = pl.ds(k * part, part)
        for e, p in enumerate(edges):
            copies.append(pltpu.make_async_copy(pops.at[:, p, rows], buf.at[:, e, rows], sem.at[2 * k + e]))
    heights = pltpu.make_async_copy(h_hbm, h, sem.at[2 * HEAD_PARTS])
    for c in copies + [heights]:
        c.start()
    heights.wait()
    hf = h[...].astype(jnp.float32)
    for p in range(width):
        row = jnp.broadcast_to(hf[p : p + 1], (SUB, ny))
        put_heights(own, p, row)
        for out, first in ((down, 0), (up, width - 2)):
            if first <= p < first + 2:
                put_rows(out, NP * nz + (p - first) * SUB, row)
    field = Field(width, nz, edge)
    for k in range(HEAD_PARTS):
        copies[2 * k].wait()
        copies[2 * k + 1].wait()
        for z in range(k * part, (k + 1) * part, SUB):
            for e, p in enumerate(edges):
                post = collide([buf[i, e, pl.ds(z, SUB), :] for i in range(Q)], 0, STEPS)
                for i in range(Q):
                    field.store(i, p, z, post[i])
                for j in range(NP):
                    if e:
                        put_rows(up, j * nz + z, post[PLUS[j]])
                    else:
                        put_rows(down, j * nz + z, post[MINUS[j]])
    give(up, down, out_a, out_b)


def inner0_kernel(width, nz, pops, own, edge, inner, out_a, out_b, rest, buf, up, down, sem):
    ny = own.shape[1]
    copy = pltpu.make_async_copy(pops.at[:, 1 : width - 1], buf, sem)
    copy.start()
    field = Field(width, nz, edge, inner)
    heights = Heights(width, own)
    copy.wait()

    def body(z):
        for p in range(1, width - 1):
            post = collide([buf[i, p - 1, pl.ds(z, SUB), :] for i in range(Q)], 0, STEPS)
            for i in range(Q):
                field.store(i, p, z, post[i])

    over_rows(nz, body)

    def body_ghost(z):
        lev = levels(z, nz, ny)
        for e, (p, comps, out) in enumerate(((width - 1, PLUS, up), (0, MINUS, down))):
            for k, i in enumerate(comps):
                put_rows(out, k * nz + z, pull(field, heights, lev, i, p, z))
            g = {i: pull(field, heights, lev, i, p, z) for i in FLAT}
            for k, row in enumerate(flat_moments(g)):
                put_rows(out, (NP + k) * nz + z, row)
            for k, i in enumerate(REST):
                put_rows(rest, (e * len(REST) + k) * nz + z, g[i])

    over_rows(nz, body_ghost)
    give(up, down, out_a, out_b)


def inner1_kernel(width, nz, own, edge, inner, rest, new_inner, out_a, out_b):
    ny = own.shape[1]
    new = Field(width, nz, None, new_inner)
    step_planes(1, STEPS, Field(width, nz, edge, inner), new, Heights(width, own), range(1, width - 1), nz, ny)
    give_second(new_inner, width, nz, out_a, out_b, rest)


def edge1_kernel(
    width, nz, own, edge0, inner0, inner1, got_a, got_b, edge1, inner2, out_a, out_b, beside, near_low, near_high
):
    ny = own.shape[1]
    take(got_a, got_b, near_low, near_high)
    for k in range(2):
        put_heights(beside, k, rows_at(near_low, NP * nz + k * SUB))
        put_heights(beside, k + 2, rows_at(near_high, NP * nz + k * SUB))
    heights = Heights(width, own, beside)
    old = Field(width, nz, edge0, inner0, near=(near_low, near_high))
    step_planes(1, STEPS, old, Field(width, nz, edge1), heights, (0, width - 1), nz, ny)
    both = Field(width, nz, edge1, inner1)
    step_planes(2, STEPS, both, Field(width, nz, None, inner2), heights, range(1, width - 1), nz, ny)
    give_second(inner2, width, nz, out_a, out_b)


def edge2_kernel(
    width,
    nz,
    own,
    beside,
    near_low,
    near_high,
    edge0,
    edge1,
    inner1,
    inner2,
    got_a,
    got_b,
    ghost1,
    sums,
    edge2,
    inner3,
    out_a,
    out_b,
    low,
    high,
):
    ny = own.shape[1]
    take(got_a, got_b, low, high)
    heights = Heights(width, own, beside)
    old = Field(width, nz, edge0, near=(near_low, near_high))
    ghost = Field(width, nz, ghost=ghost1)

    def body(z):
        lev = levels(z, nz, ny)
        for e, (p, known, mine, ref) in enumerate(((-1, PLUS, MINUS, low), (width, MINUS, PLUS, high))):
            g = {i: rows_at(ref, k * nz + z) for k, i in enumerate(known)}
            for i in mine:
                g[i] = pull(old, heights, lev, i, p, z)
            flat = [rows_at(ref, (NP + k) * nz + z) for k in range(3)]
            plus, minus = side_moments(g, PLUS), side_moments(g, MINUS)
            total = (
                flat[0] + (plus[0] + minus[0]),
                plus[0] - minus[0],
                flat[1] + (plus[1] + minus[1]),
                flat[2] + (plus[2] + minus[2]),
            )
            post = after(g, total, 1, STEPS, known + mine)
            for i in known + mine:
                ghost.store(i, p, z, post[i])
            for k, row in enumerate(total + tuple(flat)):
                put_rows(sums, (7 * e + k) * nz + z, row)

    over_rows(nz, body)
    step_planes(2, STEPS, Field(width, nz, edge1, inner1, ghost1), Field(width, nz, edge2), heights, (0, width - 1), nz, ny)
    both = Field(width, nz, edge2, inner2)
    step_planes(3, STEPS, both, Field(width, nz, None, inner3), heights, range(1, width - 1), nz, ny)
    give_second(inner3, width, nz, out_a, out_b)


def ghost_flats(width, nz, sums, low, high, flats):
    new = Field(width, nz, flats=flats)

    def body(z):
        for e, (p, ref) in enumerate(((-1, low), (width, high))):
            g = {i: rows_at(ref, (NP + k) * nz + z) for k, i in enumerate(REST)}
            row = [rows_at(sums, (7 * e + k) * nz + z) for k in range(7)]
            flat_from_rest(g, *row[4:])
            post = after(g, row[:4], 1, STEPS, FLAT)
            for i in FLAT:
                new.store(i, p, z, post[i])

    over_rows(nz, body)


def runs(comps):
    found = []
    for i in range(Q):
        if i in comps:
            continue
        if found and sum(found[-1]) == i:
            found[-1] = (found[-1][0], found[-1][1] + 1)
        else:
            found.append((i, 1))
    return found


def last_planes(field, heights, width, nz, ny, out, done, sem):
    copies = []
    for p in list(range(1, width - 1)) + [0, width - 1]:
        late = {0: PLUS, width - 1: MINUS}.get(p, [])

        def body(z, p=p, late=late):
            lev = levels(z, nz, ny)
            for i in range(Q):
                if i not in late:
                    done[i, p, pl.ds(z, SUB), :] = pull(field, heights, lev, i, p, z)

        over_rows(nz, body)
        for first, count in runs(late):
            part = pl.ds(first, count)
            copies.append(pltpu.make_async_copy(done.at[part, p], out.at[part, p], sem.at[len(copies)]))
            copies[-1].start()
    for c in copies:
        c.wait()


def enter_kernel(
    width, nz, own, beside, edge_old, edge, ghost_old, got_a, got_b, _, out, low, high, enter_low, enter_high, buf, sem
):
    ny = own.shape[1]
    heights = Heights(width, own, beside)
    copies = []
    take(got_a, got_b, low, high)
    old = Field(width, nz, edge_old, ghost=ghost_old, far=(low, high))
    ghost = (enter_low, enter_high)
    new = Field(width, nz, near=ghost)

    def body(z):
        lev = levels(z, nz, ny)
        for p, comps in ((-1, PLUS), (width, MINUS)):
            g = [pull(old, heights, lev, i, p, z) for i in range(Q)]
            post = after(g, moments(g), STEPS - 1, STEPS, comps)
            for i in comps:
                new.store(i, p, z, post[i])

    over_rows(nz, body)
    field = Field(width, nz, edge, near=ghost)
    for e, (p, comps) in enumerate(((0, PLUS), (width - 1, MINUS))):

        def enter(z, e=e, p=p, comps=comps):
            lev = levels(z, nz, ny)
            for k, i in enumerate(comps):
                buf[e, k, pl.ds(z, SUB), :] = pull(field, heights, lev, i, p, z)

        over_rows(nz, enter)
        for k, i in enumerate(comps):
            copies.append(pltpu.make_async_copy(buf.at[e, k], out.at[i, p], sem.at[len(copies)]))
            copies[-1].start()
    for c in copies:
        c.wait()


def step_kernel(s, steps, width, nz, *refs):
    refs = list(refs)

    def pop(n):
        taken = refs[:n]
        del refs[:n]
        return taken

    own, beside, edge_old, edge, inner, inner_next, ghost_old = pop(7)
    sums = pop(1)[0] if s == 2 else None
    got_a, got_b, ghost, edge_new, new = pop(5)
    out_a, out_b = pop(2) if s + 3 < steps else (None, None)
    low, high = pop(2)
    flats = pop(1)[0] if s == 2 else None
    done, sem = pop(2) if s + 2 == steps else (None, None)
    ny = own.shape[1]
    heights = Heights(width, own, beside)
    take(got_a, got_b, low, high)
    if s == 2:
        ghost_flats(width, nz, sums, low, high, flats)
    old = Field(width, nz, edge_old, ghost=ghost_old, far=(low, high), flats=flats)
    step_planes(s, steps, old, Field(width, nz, ghost=ghost), heights, (-1, width), nz, ny)
    field = Field(width, nz, edge, inner, ghost)
    step_planes(s + 1, steps, field, Field(width, nz, edge_new), heights, (0, width - 1), nz, ny)
    field = Field(width, nz, edge_new, inner_next)
    if s + 2 == steps:
        last_planes(field, heights, width, nz, ny, new, done, sem)
        return
    step_planes(s + 2, steps, field, Field(width, nz, None, new), heights, range(1, width - 1), nz, ny)
    if s + 3 < steps:
        give_second(new, width, nz, out_a, out_b)


HEAD_PARTS = 2
VMEM_LIMIT = 24 * 1024 * 1024


def per_device(pops, heights):
    _, width, nz, ny = pops.shape
    pops, heights = (pltpu.with_memory_space_constraint(x, pltpu.HBM) for x in (pops, heights))
    devices = lax.axis_size("gx")
    assert width >= 3 and nz % (HEAD_PARTS * SUB) == 0 and devices % 2 == 0 and STEPS >= 5
    pair_a = [(i, i ^ 1) for i in range(devices)]
    pair_b = [(i, (i + 1 if i % 2 else i - 1) % devices) for i in range(devices)]

    def rows(n):
        return jax.ShapeDtypeStruct((n, ny), jnp.float32)

    def scratch(n):
        return pltpu.VMEM((n, ny), jnp.float32)

    vmem = pl.BlockSpec(memory_space=pltpu.VMEM)
    hbm = pl.BlockSpec(memory_space=pltpu.HBM)
    edge_t = rows(Q * 2 * nz)
    inner_t = rows(Q * (width - 2) * nz)
    near_n = NP * nz + 2 * SUB
    sums_n = (NP + 3) * nz
    rest_n = (NP + len(REST)) * nz
    far_n = NP * nz
    dma = pltpu.SemaphoreType.DMA

    def call(kernel, args, outs, planes, scratch_shapes=(), in_specs=None, out_specs=None, **kw):
        return pl.pallas_call(
            functools.partial(kernel, width, nz),
            out_shape=outs,
            in_specs=[vmem] * len(args) if in_specs is None else in_specs,
            out_specs=[vmem] * len(outs) if out_specs is None else out_specs,
            scratch_shapes=list(scratch_shapes),
            compiler_params=pltpu.CompilerParams(vmem_limit_bytes=VMEM_LIMIT),
            cost_estimate=pl.CostEstimate(
                flops=planes * nz * ny * 250, bytes_accessed=planes * nz * ny * 4 * Q * 2, transcendentals=0
            ),
            **kw,
        )(*args)

    def exchange(a, b):
        a = lax.ppermute(a, "gx", pair_a)
        b = lax.ppermute(b, "gx", pair_b)
        return [a, b]

    edge0, a, b, own = call(
        edge0_kernel,
        [pops, heights],
        [edge_t, rows(near_n), rows(near_n), rows(3 * width * SUB)],
        2,
        [
            pltpu.VMEM((Q, 2, nz, ny), jnp.float32),
            pltpu.VMEM((width, ny), jnp.int32),
            scratch(near_n),
            scratch(near_n),
            dma((2 * HEAD_PARTS + 1,)),
        ],
        in_specs=[hbm, hbm],
    )
    near = exchange(a, b)
    inner0, a, b, rest = call(
        inner0_kernel,
        [pops, own, edge0],
        [inner_t, rows(sums_n), rows(sums_n), rows(2 * len(REST) * nz)],
        width,
        [pltpu.VMEM((Q, width - 2, nz, ny), jnp.float32), scratch(sums_n), scratch(sums_n), dma],
        in_specs=[hbm, vmem, vmem],
    )
    first = exchange(a, b)
    inner1, a, b = call(inner1_kernel, [own, edge0, inner0, rest], [inner_t, rows(rest_n), rows(rest_n)], width - 2)
    messages = {2: exchange(a, b)}
    edge1, inner2, a, b, beside, low, high = call(
        edge1_kernel,
        [own, edge0, inner0, inner1, *near],
        [edge_t, inner_t, rows(far_n), rows(far_n), rows(12 * SUB), rows(near_n), rows(near_n)],
        width,
    )
    messages[3] = exchange(a, b)
    ghost, sums, edge2, inner3, a, b = call(
        edge2_kernel,
        [own, beside, low, high, edge0, edge1, inner1, inner2, *first],
        [edge_t, rows(14 * nz), edge_t, inner_t, rows(far_n), rows(far_n)],
        width + 2,
        [scratch(sums_n), scratch(sums_n)],
    )
    messages[4] = exchange(a, b)
    edges, inners = {1: edge1, 2: edge2}, {2: inner2, 3: inner3}
    out_t = jax.ShapeDtypeStruct(pops.shape, pops.dtype)
    for s in range(2, STEPS - 1):
        args = [own, beside, edges[s - 1], edges[s], inners[s], inners[s + 1], ghost]
        outs = [edge_t, edge_t, inner_t if s + 2 < STEPS else out_t]
        n = far_n
        extra = []
        if s == 2:
            args.append(sums)
            n = rest_n
            extra = [scratch(2 * len(FLAT) * nz)]
        spaces = [vmem] * 3
        if s + 3 < STEPS:
            outs += [rows(far_n), rows(far_n)]
            spaces += [vmem] * 2
        if s + 2 == STEPS:
            spaces[2] = hbm
            copies = width - 2 + 2 * len(runs(PLUS))
            extra += [pltpu.VMEM((Q, width, nz, ny), jnp.float32), dma((copies,))]
        ghost, edges[s + 1], inners[s + 2], *given = call(
            functools.partial(step_kernel, s, STEPS),
            args + messages[s],
            outs,
            width + 2,
            [scratch(n), scratch(n)] + extra,
            out_specs=spaces,
        )
        if given:
            messages[s + 3] = exchange(*given)
    s = STEPS - 1
    args = [own, beside, edges[s - 1], edges[s], ghost] + messages[s]
    return call(
        enter_kernel,
        args + [inners[s + 1]],
        [out_t],
        2,
        [scratch(far_n)] * 4 + [pltpu.VMEM((2, NP, nz, ny), jnp.float32), dma((2 * NP,))],
        in_specs=[vmem] * len(args) + [hbm],
        out_specs=[hbm],
        input_output_aliases={len(args): 0},
    )[0]


def solution(mesh):
    placed = (P(None, ("dir", "gx"), None, None), P(("dir", "gx"), None))

    return jax.shard_map(
        per_device,
        mesh=mesh,
        in_specs=placed,
        out_specs=P(None, ("dir", "gx"), None, None),
        check_vma=False,
    )
```

```python
import functools

import jax
import jax.numpy as jnp
from jax import lax
from jax.experimental import pallas as pl
from jax.experimental.pallas import tpu as pltpu
from jax.sharding import PartitionSpec as P


STEPS = 6
Q = 19
SUB = 8

velocity_table = [
    (0, 0, 0),
    (1, 0, 0),
    (-1, 0, 0),
    (0, 1, 0),
    (0, -1, 0),
    (0, 0, 1),
    (0, 0, -1),
    (1, 1, 0),
    (-1, -1, 0),
    (1, -1, 0),
    (-1, 1, 0),
    (1, 0, 1),
    (-1, 0, -1),
    (1, 0, -1),
    (-1, 0, 1),
    (0, 1, 1),
    (0, -1, -1),
    (0, 1, -1),
    (0, -1, 1),
]
OMEGA = 1.9
KEEP = OMEGA - 1.0
MAX_HEIGHT = 32
PLUS = [1, 11, 13, 7, 9]
MINUS = [2, 12, 14, 8, 10]
FLAT = [0, 3, 4, 5, 6, 15, 16, 17, 18]
REST = [4, 6, 15, 16, 17, 18]
NP = len(PLUS)


def opp(i):
    if i == 0:
        return 0
    return i + 1 if i % 2 == 1 else i - 1


def factors(t, steps):
    if t + 1 < steps:
        return None, -OMEGA / KEEP
    scale = (-1.0 / KEEP) ** t
    return -KEEP / scale, OMEGA / scale


def moments(g):
    s = {i: g[i] + g[i + 1] for i in range(1, Q, 2)}
    d = {i: g[i] - g[i + 1] for i in range(1, Q, 2)}
    axes = (s[1] + s[3]) + s[5]
    rho = (axes + axes) + ((s[7] + s[9]) + (s[11] + s[13])) + ((s[15] + s[17]) + g[0] * 12.0)
    x = (d[1] + d[1]) + ((d[7] + d[9]) + (d[11] + d[13]))
    y = (d[3] + d[3]) + ((d[7] - d[9]) + (d[15] + d[17]))
    z = (d[5] + d[5]) + ((d[11] - d[13]) + (d[15] - d[17]))
    return rho, x, y, z


def side_moments(g, comps):
    a, b, c, d, e = (g[i] for i in comps)
    rho = (a + a) + ((b + c) + (d + e))
    return (rho, d - e, b - c) if comps is PLUS else (rho, e - d, c - b)


def flat_moments(g):
    axes = (g[3] + g[4]) + (g[5] + g[6])
    rho = (axes + axes) + ((g[15] + g[16]) + (g[17] + g[18])) + g[0] * 12.0
    a, b, y, z = g[15] - g[16], g[17] - g[18], g[3] - g[4], g[5] - g[6]
    return rho, (y + y) + (a + b), (z + z) + (a - b)


def flat_from_rest(g, rho, y, z):
    a, b = g[15] - g[16], g[17] - g[18]
    g[3] = g[4] + (y - (a + b)) * 0.5
    g[5] = g[6] + (z - (a - b)) * 0.5
    axes = (g[3] + g[4]) + (g[5] + g[6])
    g[0] = (rho - (axes + axes) - ((g[15] + g[16]) + (g[17] + g[18]))) * (1.0 / 12.0)


def terms(rho, x, y, z, rate):
    half = 1.5 / rho
    mx, my, mz = (value * (rate / 12.0) for value in (x, y, z))
    vx, vy, vz = x * half, y * half, z * half
    xx, yy, zz = mx * vx, my * vy, mz * vz
    base = rho * (rate / 36.0) - ((xx + yy) + zz) * (1.0 / 3.0)
    ex, ey, ez = base + xx, base + yy, base + zz
    mx2, my2 = mx + mx, my + my
    exy, exz, eyz = ex + yy, ex + zz, ey + zz
    xy, xz, yz = mx2 * vy, mx2 * vz, my2 * vz
    return base, {
        1: (ex, mx),
        3: (ey, my),
        5: (ez, mz),
        7: (exy + xy, mx + my),
        9: (exy - xy, mx - my),
        11: (exz + xz, mx + mz),
        13: (exz - xz, mx - mz),
        15: (eyz + yz, my + mz),
        17: (eyz - yz, my - mz),
    }


def after(g, sums, t, steps, comps=range(Q)):
    keep, rate = factors(t, steps)
    base, parts = terms(*sums, rate)
    post = {}
    for i in comps:
        own = g[i] if keep is None else g[i] * keep
        if i == 0:
            post[i] = own + base
        elif i % 2:
            post[i] = own + (parts[i][0] + parts[i][1])
        else:
            post[i] = own + (parts[i - 1][0] - parts[i - 1][1])
    return post


def collide(g, t, steps):
    return after(g, moments(g), t, steps)


class Field:
    def __init__(self, width, nz, edge=None, inner=None, ghost=None, near=None, far=None, flats=None):
        self.width, self.nz = width, nz
        self.edge, self.inner, self.ghost, self.near, self.far, self.flats = edge, inner, ghost, near, far, flats

    def place(self, i, p):
        w, nz = self.width, self.nz
        if p in (-1, w) and self.flats is not None and i in FLAT:
            return self.flats, (2 * FLAT.index(i) + (p == w)) * nz
        if p in (-1, w) and self.ghost is not None:
            return self.ghost, (2 * i + (p == w)) * nz
        if p in (-2, -1):
            return (self.near if p == -1 else self.far)[0], PLUS.index(i) * nz
        if p in (w, w + 1):
            return (self.near if p == w else self.far)[1], MINUS.index(i) * nz
        if p in (0, w - 1):
            return self.edge, (2 * i + (p != 0)) * nz
        return self.inner, (i * (w - 2) + p - 1) * nz

    def load(self, i, p, z, shift=0):
        ref, base = self.place(i, p)
        if shift:
            return ref[pl.ds(base + z - shift, SUB), :]
        return rows_at(ref, base + z)

    def store(self, i, p, z, value):
        ref, base = self.place(i, p)
        put_rows(ref, base + z, value)


def rows_at(ref, row):
    return ref[pl.ds(pl.multiple_of(row, SUB), SUB), :]


def put_rows(ref, row, value):
    ref[pl.ds(pl.multiple_of(row, SUB), SUB), :] = value


class Heights:
    def __init__(self, width, own, beside=None):
        self.width, self.own, self.beside = width, own, beside

    def get(self, p, roll):
        if 0 <= p < self.width:
            return rows_at(self.own, (3 * p + roll + 1) * SUB)
        k = p + 2 if p < 0 else p - self.width + 2
        return rows_at(self.beside, (3 * k + roll + 1) * SUB)


def roll_lanes(x, step):
    if step == 0:
        return x
    return pltpu.roll(x, step % x.shape[1], 1)


def put_heights(ref, k, row):
    for roll in (-1, 0, 1):
        put_rows(ref, (3 * k + roll + 1) * SUB, roll_lanes(row, roll))


def levels(z, nz, ny):
    at = (lax.broadcasted_iota(jnp.int32, (SUB, ny), 0) + z).astype(jnp.float32)
    top = z + SUB == nz
    return {
        0: at,
        1: at - 1.0,
        -1: jnp.where(at == nz - 1.0, -1.0, at + 1.0) if top else at + 1.0,
        "inside": at < nz - 1.0 if top else None,
    }


def pull(field, heights, lev, i, p, z):
    cx, cy, cz = velocity_table[i]
    if i == 0:
        return field.load(0, p, z)
    moved = roll_lanes(field.load(i, p - cx, z, cz), cy)
    if z - cz < MAX_HEIGHT:
        fluid = lev[cz] >= heights.get(p - cx, cy)
    elif cz == -1 and lev["inside"] is not None:
        fluid = lev["inside"]
    else:
        return moved
    return jnp.where(fluid, moved, field.load(opp(i), p, z))


def over_rows(rows, body):
    for z in range(0, rows, SUB):
        body(z)


def give(up, down, out_a, out_b):
    even = lax.rem(lax.axis_index("gx"), 2) == 0
    for cond, first, second in ((even, up, down), (jnp.logical_not(even), down, up)):

        @pl.when(cond)
        def _(first=first, second=second):
            def body(z):
                put_rows(out_a, z, rows_at(first, z))
                put_rows(out_b, z, rows_at(second, z))

            over_rows(up.shape[0], body)


def take(got_a, got_b, low, high):
    even = lax.rem(lax.axis_index("gx"), 2) == 0
    for cond, first, second in ((even, high, low), (jnp.logical_not(even), low, high)):

        @pl.when(cond)
        def _(first=first, second=second):
            def body(z):
                put_rows(first, z, rows_at(got_a, z))
                put_rows(second, z, rows_at(got_b, z))

            over_rows(low.shape[0], body)


def step_planes(t, steps, field, new, heights, planes, nz, ny):
    for p in planes:

        def body(z, p=p):
            lev = levels(z, nz, ny)
            post = collide([pull(field, heights, lev, i, p, z) for i in range(Q)], t, steps)
            for i in range(Q):
                new.store(i, p, z, post[i])

        over_rows(nz, body)


def give_second(inner, width, nz, out_a, out_b, rest=None):
    field = Field(width, nz, None, inner)

    def copy(refs, p_up, p_down):
        def body(z):
            for k in range(NP):
                put_rows(refs[0], k * nz + z, field.load(PLUS[k], p_up, z))
                put_rows(refs[1], k * nz + z, field.load(MINUS[k], p_down, z))
            if rest is not None:
                for e, ref in enumerate(refs):
                    for k in range(len(REST)):
                        put_rows(ref, (NP + k) * nz + z, rows_at(rest, (e * len(REST) + k) * nz + z))

        over_rows(nz, body)

    even = lax.rem(lax.axis_index("gx"), 2) == 0

    @pl.when(even)
    def _():
        copy((out_a, out_b), width - 2, 1)

    @pl.when(jnp.logical_not(even))
    def _():
        copy((out_b, out_a), width - 2, 1)


def first_edge(nz, side, buf, edge, copies, part):
    for k, copy in enumerate(copies):
        copy.wait()
        for z in range(k * part, (k + 1) * part, SUB):
            post = collide([buf[i, pl.ds(z, SUB), :] for i in range(Q)], 0, STEPS)
            for i in range(Q):
                put_rows(edge, (2 * i + side) * nz + z, post[i])


def near_message(width, nz, edge, own, low, out):
    for cond, comps, e, first in ((low, MINUS, 0, 0), (jnp.logical_not(low), PLUS, 1, width - 2)):

        @pl.when(cond)
        def _(comps=comps, e=e, first=first):
            for k, i in enumerate(comps):
                for z in range(0, nz, SUB):
                    put_rows(out, k * nz + z, rows_at(edge, (2 * i + e) * nz + z))
            for k in range(2):
                put_rows(out, NP * nz + k * SUB, rows_at(own, (3 * (first + k) + 1) * SUB))


def edge0_kernel(width, nz, pops, h_hbm, edge, out_b, own, buf, h, sem):
    ny = h.shape[1]
    odd = lax.rem(lax.axis_index("gx"), 2)
    plane = odd * (width - 1)
    part = nz // HEAD_PARTS
    copies = []
    for k in range(HEAD_PARTS):
        rows = pl.ds(k * part, part)
        copies.append(pltpu.make_async_copy(pops.at[:, plane, rows], buf.at[:, rows], sem.at[k]))
    heights = pltpu.make_async_copy(h_hbm, h, sem.at[HEAD_PARTS])
    for c in copies + [heights]:
        c.start()
    heights.wait()
    hf = h[...].astype(jnp.float32)
    for p in range(width):
        put_heights(own, p, jnp.broadcast_to(hf[p : p + 1], (SUB, ny)))
    first_edge(nz, odd, buf, edge, copies, part)
    near_message(width, nz, edge, own, odd == 0, out_b)


def inner0_kernel(
    width, nz, pops, own, edge_b, edge, inner, near_a, out_a, out_b, rest, buf, edge_buf, up, down, sem
):
    ny = own.shape[1]
    even = 1 - lax.rem(lax.axis_index("gx"), 2)
    copies = [
        pltpu.make_async_copy(pops.at[:, even * (width - 1)], edge_buf, sem.at[0]),
        pltpu.make_async_copy(pops.at[:, 1 : width - 1], buf, sem.at[1]),
    ]
    for c in copies:
        c.start()
    field = Field(width, nz, edge, inner)
    heights = Heights(width, own)
    first_edge(nz, even, edge_buf, edge, copies[:1], nz)
    copies[1].wait()

    def body(z):
        for p in range(1, width - 1):
            post = collide([buf[i, p - 1, pl.ds(z, SUB), :] for i in range(Q)], 0, STEPS)
            for i in range(Q):
                field.store(i, p, z, post[i])

    over_rows(nz, body)

    def body_ghost(z):
        lev = levels(z, nz, ny)
        for e, (p, comps, out) in enumerate(((width - 1, PLUS, up), (0, MINUS, down))):
            for k, i in enumerate(comps):
                put_rows(out, k * nz + z, pull(field, heights, lev, i, p, z))
            g = {i: pull(field, heights, lev, i, p, z) for i in FLAT}
            for k, row in enumerate(flat_moments(g)):
                put_rows(out, (NP + k) * nz + z, row)
            for k, i in enumerate(REST):
                put_rows(rest, (e * len(REST) + k) * nz + z, g[i])

    over_rows(nz, body_ghost)
    give(up, down, out_a, out_b)
    near_message(width, nz, edge, own, even == 0, near_a)


def inner1_kernel(width, nz, own, edge, inner, rest, new_inner, out_a, out_b):
    ny = own.shape[1]
    new = Field(width, nz, None, new_inner)
    step_planes(1, STEPS, Field(width, nz, edge, inner), new, Heights(width, own), range(1, width - 1), nz, ny)
    give_second(new_inner, width, nz, out_a, out_b, rest)


def edge1_kernel(
    width, nz, own, edge0, inner0, inner1, got_a, got_b, edge1, inner2, out_a, out_b, beside, near_low, near_high
):
    ny = own.shape[1]
    take(got_a, got_b, near_low, near_high)
    for k in range(2):
        put_heights(beside, k, rows_at(near_low, NP * nz + k * SUB))
        put_heights(beside, k + 2, rows_at(near_high, NP * nz + k * SUB))
    heights = Heights(width, own, beside)
    old = Field(width, nz, edge0, inner0, near=(near_low, near_high))
    step_planes(1, STEPS, old, Field(width, nz, edge1), heights, (0, width - 1), nz, ny)
    both = Field(width, nz, edge1, inner1)
    step_planes(2, STEPS, both, Field(width, nz, None, inner2), heights, range(1, width - 1), nz, ny)
    give_second(inner2, width, nz, out_a, out_b)


def edge2_kernel(
    width,
    nz,
    own,
    beside,
    near_low,
    near_high,
    edge0,
    edge1,
    inner1,
    inner2,
    got_a,
    got_b,
    ghost1,
    sums,
    edge2,
    inner3,
    out_a,
    out_b,
    low,
    high,
):
    ny = own.shape[1]
    take(got_a, got_b, low, high)
    heights = Heights(width, own, beside)
    old = Field(width, nz, edge0, near=(near_low, near_high))
    ghost = Field(width, nz, ghost=ghost1)

    def body(z):
        lev = levels(z, nz, ny)
        for e, (p, known, mine, ref) in enumerate(((-1, PLUS, MINUS, low), (width, MINUS, PLUS, high))):
            g = {i: rows_at(ref, k * nz + z) for k, i in enumerate(known)}
            for i in mine:
                g[i] = pull(old, heights, lev, i, p, z)
            flat = [rows_at(ref, (NP + k) * nz + z) for k in range(3)]
            plus, minus = side_moments(g, PLUS), side_moments(g, MINUS)
            total = (
                flat[0] + (plus[0] + minus[0]),
                plus[0] - minus[0],
                flat[1] + (plus[1] + minus[1]),
                flat[2] + (plus[2] + minus[2]),
            )
            post = after(g, total, 1, STEPS, known + mine)
            for i in known + mine:
                ghost.store(i, p, z, post[i])
            for k, row in enumerate(total + tuple(flat)):
                put_rows(sums, (7 * e + k) * nz + z, row)

    over_rows(nz, body)
    step_planes(2, STEPS, Field(width, nz, edge1, inner1, ghost1), Field(width, nz, edge2), heights, (0, width - 1), nz, ny)
    both = Field(width, nz, edge2, inner2)
    step_planes(3, STEPS, both, Field(width, nz, None, inner3), heights, range(1, width - 1), nz, ny)
    give_second(inner3, width, nz, out_a, out_b)


def ghost_flats(width, nz, sums, low, high, flats):
    new = Field(width, nz, flats=flats)

    def body(z):
        for e, (p, ref) in enumerate(((-1, low), (width, high))):
            g = {i: rows_at(ref, (NP + k) * nz + z) for k, i in enumerate(REST)}
            row = [rows_at(sums, (7 * e + k) * nz + z) for k in range(7)]
            flat_from_rest(g, *row[4:])
            post = after(g, row[:4], 1, STEPS, FLAT)
            for i in FLAT:
                new.store(i, p, z, post[i])

    over_rows(nz, body)


def runs(comps):
    found = []
    for i in range(Q):
        if i in comps:
            continue
        if found and sum(found[-1]) == i:
            found[-1] = (found[-1][0], found[-1][1] + 1)
        else:
            found.append((i, 1))
    return found


def last_planes(field, heights, width, nz, ny, out, done, sem):
    copies = []
    for p in list(range(1, width - 1)) + [0, width - 1]:
        late = {0: PLUS, width - 1: MINUS}.get(p, [])

        def body(z, p=p, late=late):
            lev = levels(z, nz, ny)
            for i in range(Q):
                if i not in late:
                    done[i, p, pl.ds(z, SUB), :] = pull(field, heights, lev, i, p, z)

        over_rows(nz, body)
        for first, count in runs(late):
            part = pl.ds(first, count)
            copies.append(pltpu.make_async_copy(done.at[part, p], out.at[part, p], sem.at[len(copies)]))
            copies[-1].start()
    for c in copies:
        c.wait()


def enter_kernel(
    width, nz, own, beside, edge_old, edge, ghost_old, got_a, got_b, _, out, low, high, enter_low, enter_high, buf, sem
):
    ny = own.shape[1]
    heights = Heights(width, own, beside)
    copies = []
    take(got_a, got_b, low, high)
    old = Field(width, nz, edge_old, ghost=ghost_old, far=(low, high))
    ghost = (enter_low, enter_high)
    new = Field(width, nz, near=ghost)

    def body(z):
        lev = levels(z, nz, ny)
        for p, comps in ((-1, PLUS), (width, MINUS)):
            g = [pull(old, heights, lev, i, p, z) for i in range(Q)]
            post = after(g, moments(g), STEPS - 1, STEPS, comps)
            for i in comps:
                new.store(i, p, z, post[i])

    over_rows(nz, body)
    field = Field(width, nz, edge, near=ghost)
    for e, (p, comps) in enumerate(((0, PLUS), (width - 1, MINUS))):

        def enter(z, e=e, p=p, comps=comps):
            lev = levels(z, nz, ny)
            for k, i in enumerate(comps):
                buf[e, k, pl.ds(z, SUB), :] = pull(field, heights, lev, i, p, z)

        over_rows(nz, enter)
        for k, i in enumerate(comps):
            copies.append(pltpu.make_async_copy(buf.at[e, k], out.at[i, p], sem.at[len(copies)]))
            copies[-1].start()
    for c in copies:
        c.wait()


def step_kernel(s, steps, width, nz, *refs):
    refs = list(refs)

    def pop(n):
        taken = refs[:n]
        del refs[:n]
        return taken

    own, beside, edge_old, edge, inner, inner_next, ghost_old = pop(7)
    sums = pop(1)[0] if s == 2 else None
    got_a, got_b, ghost, edge_new, new = pop(5)
    out_a, out_b = pop(2) if s + 3 < steps else (None, None)
    low, high = pop(2)
    flats = pop(1)[0] if s == 2 else None
    done, sem = pop(2) if s + 2 == steps else (None, None)
    ny = own.shape[1]
    heights = Heights(width, own, beside)
    take(got_a, got_b, low, high)
    if s == 2:
        ghost_flats(width, nz, sums, low, high, flats)
    old = Field(width, nz, edge_old, ghost=ghost_old, far=(low, high), flats=flats)
    step_planes(s, steps, old, Field(width, nz, ghost=ghost), heights, (-1, width), nz, ny)
    field = Field(width, nz, edge, inner, ghost)
    step_planes(s + 1, steps, field, Field(width, nz, edge_new), heights, (0, width - 1), nz, ny)
    field = Field(width, nz, edge_new, inner_next)
    if s + 2 == steps:
        last_planes(field, heights, width, nz, ny, new, done, sem)
        return
    step_planes(s + 2, steps, field, Field(width, nz, None, new), heights, range(1, width - 1), nz, ny)
    if s + 3 < steps:
        give_second(new, width, nz, out_a, out_b)


HEAD_PARTS = 2
VMEM_LIMIT = 24 * 1024 * 1024


def per_device(pops, heights):
    _, width, nz, ny = pops.shape
    pops, heights = (pltpu.with_memory_space_constraint(x, pltpu.HBM) for x in (pops, heights))
    devices = lax.axis_size("gx")
    assert width >= 3 and nz % (HEAD_PARTS * SUB) == 0 and devices % 2 == 0 and STEPS >= 5
    pair_a = [(i, i ^ 1) for i in range(devices)]
    pair_b = [(i, (i + 1 if i % 2 else i - 1) % devices) for i in range(devices)]

    def rows(n):
        return jax.ShapeDtypeStruct((n, ny), jnp.float32)

    def scratch(n):
        return pltpu.VMEM((n, ny), jnp.float32)

    vmem = pl.BlockSpec(memory_space=pltpu.VMEM)
    hbm = pl.BlockSpec(memory_space=pltpu.HBM)
    edge_t = rows(Q * 2 * nz)
    inner_t = rows(Q * (width - 2) * nz)
    near_n = NP * nz + 2 * SUB
    sums_n = (NP + 3) * nz
    rest_n = (NP + len(REST)) * nz
    far_n = NP * nz
    dma = pltpu.SemaphoreType.DMA

    def call(kernel, args, outs, planes, scratch_shapes=(), in_specs=None, out_specs=None, **kw):
        return pl.pallas_call(
            functools.partial(kernel, width, nz),
            out_shape=outs,
            in_specs=[vmem] * len(args) if in_specs is None else in_specs,
            out_specs=[vmem] * len(outs) if out_specs is None else out_specs,
            scratch_shapes=list(scratch_shapes),
            compiler_params=pltpu.CompilerParams(vmem_limit_bytes=VMEM_LIMIT),
            cost_estimate=pl.CostEstimate(
                flops=planes * nz * ny * 250, bytes_accessed=planes * nz * ny * 4 * Q * 2, transcendentals=0
            ),
            **kw,
        )(*args)

    def exchange(a, b):
        a = lax.ppermute(a, "gx", pair_a)
        b = lax.ppermute(b, "gx", pair_b)
        return [a, b]

    edge0, near_b, own = call(
        edge0_kernel,
        [pops, heights],
        [edge_t, rows(near_n), rows(3 * width * SUB)],
        1,
        [pltpu.VMEM((Q, nz, ny), jnp.float32), pltpu.VMEM((width, ny), jnp.int32), dma((HEAD_PARTS + 1,))],
        in_specs=[hbm, hbm],
    )
    edge0, inner0, near_a, a, b, rest = call(
        inner0_kernel,
        [pops, own, edge0],
        [edge_t, inner_t, rows(near_n), rows(sums_n), rows(sums_n), rows(2 * len(REST) * nz)],
        width,
        [
            pltpu.VMEM((Q, width - 2, nz, ny), jnp.float32),
            pltpu.VMEM((Q, nz, ny), jnp.float32),
            scratch(sums_n),
            scratch(sums_n),
            dma((2,)),
        ],
        in_specs=[hbm, vmem, vmem],
        input_output_aliases={2: 0},
    )
    near = exchange(near_a, near_b)
    first = exchange(a, b)
    inner1, a, b = call(inner1_kernel, [own, edge0, inner0, rest], [inner_t, rows(rest_n), rows(rest_n)], width - 2)
    messages = {2: exchange(a, b)}
    edge1, inner2, a, b, beside, low, high = call(
        edge1_kernel,
        [own, edge0, inner0, inner1, *near],
        [edge_t, inner_t, rows(far_n), rows(far_n), rows(12 * SUB), rows(near_n), rows(near_n)],
        width,
    )
    messages[3] = exchange(a, b)
    ghost, sums, edge2, inner3, a, b = call(
        edge2_kernel,
        [own, beside, low, high, edge0, edge1, inner1, inner2, *first],
        [edge_t, rows(14 * nz), edge_t, inner_t, rows(far_n), rows(far_n)],
        width + 2,
        [scratch(sums_n), scratch(sums_n)],
    )
    messages[4] = exchange(a, b)
    edges, inners = {1: edge1, 2: edge2}, {2: inner2, 3: inner3}
    out_t = jax.ShapeDtypeStruct(pops.shape, pops.dtype)
    for s in range(2, STEPS - 1):
        args = [own, beside, edges[s - 1], edges[s], inners[s], inners[s + 1], ghost]
        outs = [edge_t, edge_t, inner_t if s + 2 < STEPS else out_t]
        n = far_n
        extra = []
        if s == 2:
            args.append(sums)
            n = rest_n
            extra = [scratch(2 * len(FLAT) * nz)]
        spaces = [vmem] * 3
        if s + 3 < STEPS:
            outs += [rows(far_n), rows(far_n)]
            spaces += [vmem] * 2
        if s + 2 == STEPS:
            spaces[2] = hbm
            copies = width - 2 + 2 * len(runs(PLUS))
            extra += [pltpu.VMEM((Q, width, nz, ny), jnp.float32), dma((copies,))]
        ghost, edges[s + 1], inners[s + 2], *given = call(
            functools.partial(step_kernel, s, STEPS),
            args + messages[s],
            outs,
            width + 2,
            [scratch(n), scratch(n)] + extra,
            out_specs=spaces,
        )
        if given:
            messages[s + 3] = exchange(*given)
    s = STEPS - 1
    args = [own, beside, edges[s - 1], edges[s], ghost] + messages[s]
    return call(
        enter_kernel,
        args + [inners[s + 1]],
        [out_t],
        2,
        [scratch(far_n)] * 4 + [pltpu.VMEM((2, NP, nz, ny), jnp.float32), dma((2 * NP,))],
        in_specs=[vmem] * len(args) + [hbm],
        out_specs=[hbm],
        input_output_aliases={len(args): 0},
    )[0]


def solution(mesh):
    placed = (P(None, ("dir", "gx"), None, None), P(("dir", "gx"), None))

    return jax.shard_map(
        per_device,
        mesh=mesh,
        in_specs=placed,
        out_specs=P(None, ("dir", "gx"), None, None),
        check_vma=False,
    )
```
